32 devices in a mesh: row: 8 (over z, core), col: 4 (over y, x).
Axes of the slice: x: 2, y: 2, z: 4, core: 2. Of those that a mesh axis runs over, the one named last changes fastest.
Arguments:
- queries: bfloat16 [256, 32, 1536], P('row', 'col'), may hold values from -24 to 24
- keys: bfloat16 [256, 32, 1536], P('row', 'col'), may hold values from -24 to 24
- values: bfloat16 [256, 32, 1536], P('row', 'col'), may hold values from -12 to 12
- memory_bias: float32 [12], replicated, may hold values from 1 to 6
Outputs:
- attended: bfloat16 [256, 32, 1536], P('row', 'col')
The draws below stay inside these ranges and needn't reach their ends.
All inputs are finite; a program needn't handle non-finite values.
Results may differ from the reference program's by a relative error of at most 0.0048.
Values may be sent and summed in bfloat16 or wider, within the bound.
No kernel may reach another device: no remote copies, remote signals or barrier semaphores. Data moves between devices by JAX's collectives and lax.ppermute only.
A program may use at most 64 MiB of HBM per device.

```python
import jax
import jax.numpy as jnp
from jax import lax

D = 1536
HEADS = 12
HD = 128
ROW_DEV = 32
CD = 8
ROWS = 256
COLS = 32
N_ROW = 8
N_COL = 4


def region_offset(key, spread, limit):
    offsets = jnp.clip(spread * jax.random.normal(key, (N_ROW, 1, N_COL, 1, D), jnp.float32), -limit, limit)
    offsets = jnp.broadcast_to(offsets, (N_ROW, ROW_DEV, N_COL, CD, D))
    return offsets.reshape(ROWS, COLS, D)


def drawn_pair(key):
    query_key = jax.random.fold_in(key, 11)
    other_key = jax.random.fold_in(key, 12)
    offset_key = jax.random.fold_in(key, 14)
    full_shape = (ROWS, COLS, D)
    key_offset = region_offset(offset_key, 0.6, 2.4)
    query_all = jnp.clip(1.5 * jax.random.normal(query_key, full_shape, jnp.float32), -9.0, 9.0)
    key_all = jnp.clip(jax.random.normal(other_key, full_shape, jnp.float32), -6.0, 6.0) + key_offset
    return (query_all, key_all)


def draw_queries(key, part):
    return drawn_pair(key)[0].astype(jnp.bfloat16)


def draw_keys(key, part):
    return drawn_pair(key)[1].astype(jnp.bfloat16)


def draw_values(key, part):
    noise_key = jax.random.fold_in(key, 21)
    offset_key = jax.random.fold_in(key, 22)
    full_shape = (ROWS, COLS, D)
    value_offset = region_offset(offset_key, 1.0, 3.0)
    noise = jnp.clip(2.0 * jax.random.normal(noise_key, full_shape, jnp.float32), -8.0, 8.0)
    return (noise + value_offset).astype(jnp.bfloat16)


def setup_inputs(seed: int = 0) -> dict:
    arg_keys = jax.random.split(jax.random.key(seed), 5)
    return {
        "queries": draw_queries(jax.random.fold_in(arg_keys[4], 71), 0),
        "keys": draw_keys(jax.random.fold_in(arg_keys[4], 71), 0),
        "values": draw_values(jax.random.fold_in(arg_keys[4], 71), 0),
        "memory_bias": jnp.clip(jax.random.uniform(arg_keys[3], (HEADS,), jnp.float32, 1.0, 6.0), 1.0, 6.0),
    }


def region_means(tensor):
    grouped = tensor.astype(jnp.float32).reshape(N_ROW, ROW_DEV, N_COL, CD, D)
    pooled = jnp.mean(grouped, axis=(1, 3)).astype(jnp.bfloat16)
    pooled = lax.optimization_barrier(pooled)
    return pooled.astype(jnp.float32).reshape(N_ROW, N_COL, HEADS, HD)


def reference(queries, keys, values, memory_bias):
    memory_keys = region_means(keys)
    memory_values = region_means(values)
    score_scale = 1.0 / (HD ** 0.5)

    def column(index):
        query_col = lax.dynamic_index_in_dim(queries, index, 1, keepdims=False).astype(jnp.float32).reshape(ROWS, HEADS, HD)
        key_col = lax.dynamic_index_in_dim(keys, index, 1, keepdims=False).astype(jnp.float32).reshape(ROWS, HEADS, HD)
        value_col = lax.dynamic_index_in_dim(values, index, 1, keepdims=False).astype(jnp.float32).reshape(ROWS, HEADS, HD)
        col_scores = jnp.einsum("rhe,she->hrs", query_col, key_col) * score_scale
        query_band = query_col.reshape(N_ROW, ROW_DEV, HEADS, HD)
        mem_scores = jnp.einsum("brhe,bnhe->hbrn", query_band, memory_keys) * score_scale
        mem_scores = mem_scores + memory_bias[:, None, None, None]
        mem_scores = mem_scores.reshape(HEADS, ROWS, N_COL)
        peak_score = jnp.maximum(jnp.max(col_scores, axis=-1, keepdims=True), jnp.max(mem_scores, axis=-1, keepdims=True))
        col_exp = jnp.exp(col_scores - peak_score)
        mem_exp = jnp.exp(mem_scores - peak_score)
        total_weight = jnp.sum(col_exp, axis=-1, keepdims=True) + jnp.sum(mem_exp, axis=-1, keepdims=True)
        col_weights = lax.optimization_barrier((col_exp / total_weight).astype(jnp.bfloat16)).astype(jnp.float32)
        mem_weights = lax.optimization_barrier((mem_exp / total_weight).astype(jnp.bfloat16)).astype(jnp.float32)
        mixed = jnp.einsum("hrs,she->rhe", col_weights, value_col)
        mem_band = mem_weights.reshape(HEADS, N_ROW, ROW_DEV, N_COL)
        mixed = mixed + jnp.einsum("hbrn,bnhe->brhe", mem_band, memory_values).reshape(ROWS, HEADS, HD)
        return mixed.reshape(ROWS, D).astype(jnp.bfloat16)

    columns_out = lax.map(column, jnp.arange(COLS, dtype=jnp.int32))
    return jnp.transpose(columns_out, (1, 0, 2))
```

```python
import functools
import math

import jax
import jax.numpy as jnp
from jax import lax
from jax.experimental import pallas as pl
from jax.experimental.pallas import tpu as pltpu
from jax.sharding import PartitionSpec as P

LOG2E = 1.4426950408889634
VMEM_LIMIT = 48 * 1024 * 1024


def spread_kernel(dims, head_ids, me_ref, q_ref, k_ref, v_ref, *rest):
    n_row, col_groups, cols_g, heads_g, row_dev, col_dev, head_dim = dims
    out_refs = rest[:n_row]
    wide, blocks, sems = rest[n_row:]
    me = me_ref[0]
    slot = 0
    for t, ref in enumerate((q_ref, k_ref, v_ref)):
        for g in range(n_row // col_groups):
            for j, local in enumerate(head_ids):
                start = (g * heads_g + local) * head_dim
                wide[slot] = (
                    ref[:, :, start : start + head_dim]
                    .astype(jnp.float32)
                    .reshape(row_dev * col_dev, head_dim)
                )
                for c in range(col_dev):
                    dest = g * col_groups + c // cols_g
                    pair = j * cols_g + c % cols_g
                    blocks[dest, t, pair] = wide[slot, pl.ds(c, row_dev, stride=col_dev), :].astype(
                        jnp.bfloat16
                    )
                slot = (slot + 1) % wide.shape[0]
    copies = [
        pltpu.make_async_copy(blocks.at[me ^ k], out_refs[k], sems.at[k]) for k in range(n_row)
    ]
    for copy in copies:
        copy.start()
    for copy in copies:
        copy.wait()


def spread(dims, head_ids, me, q, k, v):
    n_row, col_groups, cols_g, heads_g, row_dev, col_dev, head_dim = dims
    block = (3, len(head_ids) * cols_g, row_dev, head_dim)
    return pl.pallas_call(
        functools.partial(spread_kernel, dims, head_ids),
        out_shape=[jax.ShapeDtypeStruct(block, jnp.bfloat16)] * n_row,
        in_specs=[pl.BlockSpec(memory_space=pltpu.SMEM)]
        + [pl.BlockSpec(memory_space=pltpu.VMEM)] * 3,
        out_specs=[pl.BlockSpec(memory_space=pl.ANY)] * n_row,
        scratch_shapes=[
            pltpu.VMEM((4, row_dev * col_dev, head_dim), jnp.float32),
            pltpu.VMEM((n_row,) + block, jnp.bfloat16),
            pltpu.SemaphoreType.DMA((n_row,)),
        ],
        compiler_params=pltpu.CompilerParams(vmem_limit_bytes=VMEM_LIMIT),
        name="spread",
    )(me, q, k, v)


def attend_kernel(dims, n_col, head_ids, me_ref, bias_ref, mem_ref, *rest):
    n_row, col_groups, cols_g, heads_g, row_dev, col_dev, head_dim = dims
    in_refs, out_refs = rest[:n_row], rest[n_row:]
    rows, slots = n_row * row_dev, n_row * n_col
    me = me_ref[0]
    scale = LOG2E / math.sqrt(head_dim)
    band = (lax.broadcasted_iota(jnp.int32, (rows, slots), 0) // row_dev) ^ me
    owner = lax.broadcasted_iota(jnp.int32, (rows, slots), 1) // n_col
    hidden = jnp.where(band == owner, 0.0, -1e30)
    ones = jnp.ones((rows, head_dim), jnp.bfloat16)
    slot_ones = jnp.ones((slots, head_dim), jnp.bfloat16)
    nt = (((1,), (1,)), ((), ()))
    group = me // col_groups
    for j, local in enumerate(head_ids):
        bias = bias_ref[group * heads_g + local] * LOG2E
        shift = hidden + bias
        mem_key = mem_ref[0, local]
        mem_value = jnp.concatenate([mem_ref[1, local], slot_ones], axis=1)
        for c in range(cols_g):
            pair = j * cols_g + c
            query = jnp.concatenate([ref[0, pair] for ref in in_refs], axis=0)
            key = jnp.concatenate([ref[1, pair] for ref in in_refs], axis=0)
            value = jnp.concatenate([ref[2, pair] for ref in in_refs], axis=0)
            value = jnp.concatenate([value, ones], axis=1)
            col = lax.dot_general(query, key, nt, preferred_element_type=jnp.float32) * scale
            mem = lax.dot_general(query, mem_key, nt, preferred_element_type=jnp.float32) * scale
            mem = mem + shift
            peak = jnp.maximum(
                jnp.max(col, axis=1, keepdims=True), jnp.max(mem, axis=1, keepdims=True)
            )
            col = jnp.exp2(col - peak).astype(jnp.bfloat16)
            mem = jnp.exp2(mem - peak).astype(jnp.bfloat16)
            mixed = jnp.dot(col, value, preferred_element_type=jnp.float32)
            mixed = mixed + jnp.dot(mem, mem_value, preferred_element_type=jnp.float32)
            out = (mixed[:, :head_dim] / mixed[:, head_dim:]).astype(jnp.bfloat16)
            for k in range(n_row):
                out_refs[k][pair] = out[k * row_dev : (k + 1) * row_dev]


def attend(dims, n_col, head_ids, me, bias, mem, blocks):
    n_row, col_groups, cols_g, heads_g, row_dev, col_dev, head_dim = dims
    block = (len(head_ids) * cols_g, row_dev, head_dim)
    return pl.pallas_call(
        functools.partial(attend_kernel, dims, n_col, head_ids),
        out_shape=[jax.ShapeDtypeStruct(block, jnp.bfloat16)] * n_row,
        in_specs=[pl.BlockSpec(memory_space=pltpu.SMEM)] * 2
        + [pl.BlockSpec(memory_space=pltpu.VMEM)] * (1 + n_row),
        out_specs=[pl.BlockSpec(memory_space=pltpu.VMEM)] * n_row,
        compiler_params=pltpu.CompilerParams(vmem_limit_bytes=VMEM_LIMIT),
        name="attend",
    )(me, bias, mem, *blocks)


def collect_kernel(dims, chunks, me_ref, *rest):
    n_row, col_groups, cols_g, heads_g, row_dev, col_dev, head_dim = dims
    in_refs = rest[: n_row * len(chunks)]
    out_ref, *held, wide = rest[n_row * len(chunks) :]
    me = me_ref[0]
    for i in range(len(chunks)):
        for k in range(n_row):
            held[i][me ^ k] = in_refs[i * n_row + k][...]
    slot = 0
    for i, head_ids in enumerate(chunks):
        for g in range(n_row // col_groups):
            for j, local in enumerate(head_ids):
                for c in range(col_dev):
                    dest = g * col_groups + c // cols_g
                    pair = j * cols_g + c % cols_g
                    wide[slot, pl.ds(c, row_dev, stride=col_dev), :] = held[i][dest, pair].astype(
                        jnp.float32
                    )
                start = (g * heads_g + local) * head_dim
                out_ref[:, :, start : start + head_dim] = (
                    wide[slot].astype(jnp.bfloat16).reshape(row_dev, col_dev, head_dim)
                )
                slot = (slot + 1) % wide.shape[0]


def collect(dims, chunks, me, blocks):
    n_row, col_groups, cols_g, heads_g, row_dev, col_dev, head_dim = dims
    width = n_row // col_groups * heads_g * head_dim
    return pl.pallas_call(
        functools.partial(collect_kernel, dims, chunks),
        out_shape=jax.ShapeDtypeStruct((row_dev, col_dev, width), jnp.bfloat16),
        in_specs=[pl.BlockSpec(memory_space=pltpu.SMEM)]
        + [pl.BlockSpec(memory_space=pltpu.VMEM)] * len(blocks),
        out_specs=pl.BlockSpec(memory_space=pltpu.VMEM),
        scratch_shapes=[
            pltpu.VMEM((n_row, len(ids) * cols_g, row_dev, head_dim), jnp.bfloat16)
            for ids in chunks
        ]
        + [pltpu.VMEM((4, row_dev * col_dev, head_dim), jnp.float32)],
        compiler_params=pltpu.CompilerParams(vmem_limit_bytes=VMEM_LIMIT),
        name="collect",
    )(me, *blocks)


def exchange(blocks):
    n_row = len(blocks)
    return [blocks[0]] + [
        lax.ppermute(blocks[k], "row", [(i, i ^ k) for i in range(n_row)]) for k in range(1, n_row)
    ]


def per_device(queries, keys, values, memory_bias):
    row_dev, col_dev, model_width = queries.shape
    n_row = lax.axis_size("row")
    n_col = lax.axis_size("col")
    head_count = memory_bias.shape[0]
    head_dim = model_width // head_count
    head_groups = math.gcd(head_count, n_row)
    col_groups = n_row // head_groups
    heads_g = head_count // head_groups
    cols_g = col_dev // col_groups
    dims = (n_row, col_groups, cols_g, heads_g, row_dev, col_dev, head_dim)
    split = max(1, heads_g * 2 // 3)
    chunks = [tuple(range(split)), tuple(range(split, heads_g))]
    me = lax.axis_index("row").astype(jnp.int32).reshape(1)

    sent = [spread(dims, ids, me, queries, keys, values) for ids in chunks]
    arrived = [exchange(blocks) for blocks in sent]

    own_keys = jnp.mean(keys, axis=(0, 1), dtype=jnp.float32).astype(jnp.bfloat16)
    own_values = jnp.mean(values, axis=(0, 1), dtype=jnp.float32).astype(jnp.bfloat16)
    own = jnp.stack([own_keys, own_values])[None]
    band = lax.all_gather(own, "col", axis=0, tiled=True)
    band = band.reshape(n_col, 2, head_groups, 1, heads_g, head_dim)
    band = jnp.transpose(band, (2, 3, 1, 4, 0, 5))
    band = jnp.broadcast_to(band, (head_groups, col_groups, 2, heads_g, n_col, head_dim))
    band = band.reshape(n_row, 2 * heads_g * n_col, head_dim)
    mem = lax.all_to_all(band, "row", split_axis=0, concat_axis=0, tiled=True)
    mem = mem.reshape(n_row, 2, heads_g, n_col, head_dim)
    mem = jnp.transpose(mem, (1, 2, 0, 3, 4)).reshape(2, heads_g, n_row * n_col, head_dim)

    returned = []
    for ids, blocks in zip(chunks, arrived):
        returned += exchange(attend(dims, n_col, ids, me, memory_bias, mem, blocks))
    return collect(dims, chunks, me, returned)


def solution(mesh):
    return jax.shard_map(
        per_device,
        mesh=mesh,
        in_specs=(P("row", "col", None), P("row", "col", None), P("row", "col", None), P()),
        out_specs=P("row", "col", None),
        check_vma=False,
    )
```

```python
import functools
import math

import jax
import jax.numpy as jnp
from jax import lax
from jax.experimental import pallas as pl
from jax.experimental.pallas import tpu as pltpu
from jax.sharding import PartitionSpec as P


LOG2E = 1.4426950408889634
PARTS = 3
NT = (((1,), (1,)), ((), ()))
PARAMS = pltpu.CompilerParams(vmem_limit_bytes=20 * 1024 * 1024)
SMEM = pl.BlockSpec(memory_space=pltpu.SMEM)
VMEM = pl.BlockSpec(memory_space=pltpu.VMEM)
HBM = pl.BlockSpec(memory_space=pltpu.HBM)


def in_hbm(x):
    return pltpu.with_memory_space_constraint(x, pltpu.HBM)


class Dims:
    def __init__(self, n_row, n_col, heads, head_dim, row_dev, col_dev):
        self.n_row, self.n_col, self.head_dim = n_row, n_col, head_dim
        self.row_dev, self.col_dev, self.heads = row_dev, col_dev, heads
        self.head_groups = math.gcd(heads, n_row)
        self.col_groups = n_row // self.head_groups
        self.heads_g = heads // self.head_groups
        self.cols_g = col_dev // self.col_groups
        self.pairs = self.heads_g * self.cols_g
        self.width = self.heads_g * head_dim
        self.patches = row_dev * col_dev
        self.rows = n_row * row_dev
        self.sent_rows = 3 * self.pairs * row_dev
        self.back_rows = (self.pairs + 1) * row_dev

    def lane(self, me, kg):
        return pl.multiple_of(((me // self.col_groups) ^ kg) * self.width, 128)

    def column(self, me, kl, c):
        return ((me % self.col_groups) ^ kl) * self.cols_g + c


def spread_kernel(dims, kgs, me_ref, *refs):
    args, outs, (raw, wide, sems) = refs[:3], refs[3:-3], refs[-3:]
    me, head_dim, row_dev = me_ref[0], dims.head_dim, dims.row_dev
    loads = {}
    for i, kg in enumerate(kgs):
        for t, arg in enumerate(args):
            loads[i, t] = pltpu.make_async_copy(
                arg.at[:, :, pl.ds(dims.lane(me, kg), dims.width)], raw.at[i, t], sems.at[i, t]
            )
            loads[i, t].start()
    slot = 0
    for i in range(len(kgs)):
        for t in range(3):
            loads[i, t].wait()
            for j in range(dims.heads_g):
                wide[slot] = (
                    raw[i, t, :, :, j * head_dim : (j + 1) * head_dim]
                    .astype(jnp.float32)
                    .reshape(dims.patches, head_dim)
                )
                for kl in range(dims.col_groups):
                    for c in range(dims.cols_g):
                        at = (t * dims.pairs + j * dims.cols_g + c) * row_dev
                        outs[i * dims.col_groups + kl][at : at + row_dev] = wide[
                            slot,
                            pl.ds(dims.column(me, kl, c), row_dev, stride=dims.col_dev),
                            :,
                        ].astype(jnp.bfloat16)
                slot = (slot + 1) % wide.shape[0]


def spread(dims, kgs, me, args):
    block = jax.ShapeDtypeStruct((dims.sent_rows, dims.head_dim), jnp.bfloat16)
    count = len(kgs) * dims.col_groups
    return pl.pallas_call(
        functools.partial(spread_kernel, dims, kgs),
        out_shape=[block] * count,
        in_specs=[SMEM] + [HBM] * 3,
        out_specs=[VMEM] * count,
        scratch_shapes=[
            pltpu.VMEM((len(kgs), 3, dims.row_dev, dims.col_dev, dims.width), jnp.bfloat16),
            pltpu.VMEM((4, dims.patches, dims.head_dim), jnp.float32),
            pltpu.SemaphoreType.DMA((len(kgs), 3)),
        ],
        compiler_params=PARAMS,
        name="spread",
    )(me, *[in_hbm(arg) for arg in args])


def pool_kernel(dims, k_ref, v_ref, out_ref, raw, sems):
    loads = [
        pltpu.make_async_copy(ref, raw.at[i], sems.at[i]) for i, ref in enumerate((k_ref, v_ref))
    ]
    for load in loads:
        load.start()
    for i, load in enumerate(loads):
        load.wait()
        total = jnp.zeros((dims.col_dev, raw.shape[-1]), jnp.float32)
        for r in range(dims.row_dev):
            total = total + raw[i, r].astype(jnp.float32)
        mean = jnp.sum(total, axis=0, keepdims=True) * (1.0 / dims.patches)
        out_ref[i : i + 1] = mean.astype(jnp.bfloat16).astype(jnp.float32)


def pool(dims, keys, values):
    return pl.pallas_call(
        functools.partial(pool_kernel, dims),
        out_shape=jax.ShapeDtypeStruct((2, keys.shape[-1]), jnp.float32),
        in_specs=[HBM] * 2,
        out_specs=VMEM,
        scratch_shapes=[
            pltpu.VMEM((2,) + keys.shape, jnp.bfloat16),
            pltpu.SemaphoreType.DMA((2,)),
        ],
        compiler_params=PARAMS,
        name="pool",
    )(in_hbm(keys), in_hbm(values)).astype(jnp.bfloat16)


def recall_kernel(dims, bias_ref, q_ref, key_ref, value_ref, out_ref, lse_ref, raw, sem):
    load = pltpu.make_async_copy(q_ref, raw, sem)
    load.start()
    load.wait()
    head_dim = dims.head_dim
    scale = LOG2E / math.sqrt(head_dim)
    ones = jnp.ones((dims.n_col, head_dim), jnp.bfloat16)
    for h in range(dims.heads):
        lanes = slice(h * head_dim, (h + 1) * head_dim)
        query = raw[:, :, lanes].reshape(dims.patches, head_dim)
        value = jnp.concatenate([value_ref[:, lanes], ones], axis=1)
        score = lax.dot_general(query, key_ref[:, lanes], NT, preferred_element_type=jnp.float32)
        score = score * scale + bias_ref[h] * LOG2E
        peak = jnp.max(score, axis=1, keepdims=True)
        weight = jnp.exp2(score - peak).astype(jnp.bfloat16)
        mixed = jnp.dot(weight, value, preferred_element_type=jnp.float32)
        total = mixed[:, head_dim:]
        out_ref[:, lanes] = mixed[:, :head_dim] / total
        lse_ref[:, lanes] = peak + jnp.log2(total)


def recall(dims, bias, queries, key, value):
    out = jax.ShapeDtypeStruct((dims.patches, queries.shape[-1]), jnp.float32)
    return pl.pallas_call(
        functools.partial(recall_kernel, dims),
        out_shape=[out] * 2,
        in_specs=[SMEM, HBM] + [VMEM] * 2,
        out_specs=[VMEM] * 2,
        scratch_shapes=[pltpu.VMEM(queries.shape, jnp.bfloat16), pltpu.SemaphoreType.DMA],
        compiler_params=PARAMS,
        name="recall",
    )(bias, in_hbm(queries), key, value)


def attend_kernel(dims, ks, *refs):
    ins, outs = refs[: dims.n_row], refs[dims.n_row :]
    row_dev, head_dim, rows = dims.row_dev, dims.head_dim, dims.rows
    count = len(ks) * row_dev
    scale = LOG2E / math.sqrt(head_dim)
    ones = jnp.ones((rows, head_dim), jnp.bfloat16)
    lane = lax.broadcasted_iota(jnp.int32, (count, head_dim), 1)
    tail = jnp.zeros((count, head_dim), jnp.float32)

    def gather(t, pair, sources):
        at = (t * dims.pairs + pair) * row_dev
        return jnp.concatenate([ins[k][at : at + row_dev] for k in sources], axis=0)

    for pair in range(dims.pairs):
        query = gather(0, pair, ks)
        key = gather(1, pair, range(dims.n_row))
        value = jnp.concatenate([gather(2, pair, range(dims.n_row)), ones], axis=1)
        score = lax.dot_general(query, key, NT, preferred_element_type=jnp.float32) * scale
        peak = jnp.max(score, axis=1, keepdims=True)
        weight = jnp.exp2(score - peak).astype(jnp.bfloat16)
        mixed = jnp.dot(weight, value, preferred_element_type=jnp.float32)
        total = mixed[:, head_dim:]
        out = (mixed[:, :head_dim] / total).astype(jnp.bfloat16)
        rest = peak + jnp.log2(total)
        for part in range(PARTS):
            term = rest.astype(jnp.bfloat16).astype(jnp.float32)
            tail = jnp.where(lane == pair * PARTS + part, term, tail)
            rest = rest - term
        for i in range(len(ks)):
            outs[i][pair * row_dev : (pair + 1) * row_dev] = out[i * row_dev : (i + 1) * row_dev]
    tail = tail.astype(jnp.bfloat16)
    for i in range(len(ks)):
        outs[i][dims.pairs * row_dev :] = tail[i * row_dev : (i + 1) * row_dev]


def attend(dims, ks, blocks):
    block = jax.ShapeDtypeStruct((dims.back_rows, dims.head_dim), jnp.bfloat16)
    return pl.pallas_call(
        functools.partial(attend_kernel, dims, ks),
        out_shape=[block] * len(ks),
        in_specs=[VMEM] * dims.n_row,
        out_specs=[VMEM] * len(ks),
        compiler_params=PARAMS,
        name="attend",
    )(*blocks)


def collect_kernel(dims, kgs, me_ref, mem_ref, lse_ref, *refs):
    blocks = refs[: len(kgs) * dims.col_groups]
    out, wide, wide_lse, done, sems = refs[-5:]
    me, head_dim, row_dev = me_ref[0], dims.head_dim, dims.row_dev
    row = lax.broadcasted_iota(jnp.int32, (head_dim, dims.pairs * head_dim), 0)
    col = lax.broadcasted_iota(jnp.int32, (head_dim, dims.pairs * head_dim), 1)
    pick = jnp.where(row // PARTS == col // head_dim, 1.0, 0.0).astype(jnp.bfloat16)
    stores = []
    slot = 0
    for i, kg in enumerate(kgs):
        mine = blocks[i * dims.col_groups : (i + 1) * dims.col_groups]
        tails = [ref[dims.pairs * row_dev :] for ref in mine]
        tails = jnp.concatenate(tails, axis=0)
        lses = jnp.dot(tails, pick, preferred_element_type=jnp.float32)
        lane = dims.lane(me, kg)
        for j in range(dims.heads_g):
            for kl, ref in enumerate(mine):
                for c in range(dims.cols_g):
                    pair = j * dims.cols_g + c
                    to = pl.ds(dims.column(me, kl, c), row_dev, stride=dims.col_dev)
                    wide[slot, to, :] = ref[pair * row_dev : (pair + 1) * row_dev].astype(
                        jnp.float32
                    )
                    wide_lse[slot, to, :] = lses[
                        kl * row_dev : (kl + 1) * row_dev, pair * head_dim : (pair + 1) * head_dim
                    ]
            at = pl.ds(pl.multiple_of(lane + j * head_dim, 128), head_dim)
            mem = mem_ref[:, at]
            share = 1.0 / (1.0 + jnp.exp2(lse_ref[:, at] - wide_lse[slot]))
            value = mem + share * (wide[slot] - mem)
            done[i, :, :, j * head_dim : (j + 1) * head_dim] = value.astype(jnp.bfloat16).reshape(
                row_dev, dims.col_dev, head_dim
            )
            slot = (slot + 1) % wide.shape[0]
        stores.append(
            pltpu.make_async_copy(
                done.at[i], out.at[:, :, pl.ds(lane, dims.width)], sems.at[i]
            )
        )
        stores[-1].start()
    for store in stores:
        store.wait()


def collect(dims, kgs, me, mem, lse, blocks, out=None):
    shape = (dims.row_dev, dims.col_dev, dims.heads * dims.head_dim)
    operands = (me, mem, lse, *blocks) + (() if out is None else (out,))
    return pl.pallas_call(
        functools.partial(collect_kernel, dims, kgs),
        out_shape=jax.ShapeDtypeStruct(shape, jnp.bfloat16),
        in_specs=[SMEM] + [VMEM] * (2 + len(blocks)) + [HBM] * (out is not None),
        out_specs=HBM,
        scratch_shapes=[
            pltpu.VMEM((4, dims.patches, dims.head_dim), jnp.float32),
            pltpu.VMEM((4, dims.patches, dims.head_dim), jnp.float32),
            pltpu.VMEM((len(kgs),) + shape[:2] + (dims.width,), jnp.bfloat16),
            pltpu.SemaphoreType.DMA((len(kgs),)),
        ],
        input_output_aliases={} if out is None else {len(operands) - 1: 0},
        compiler_params=PARAMS,
        name="collect",
    )(*operands)


def exchange(dims, ks, blocks):
    return [
        lax.ppermute(block, "row", [(i, i ^ k) for i in range(dims.n_row)]) if k else block
        for k, block in zip(ks, blocks)
    ]


def per_device(queries, keys, values, memory_bias):
    row_dev, col_dev, model_width = queries.shape
    n_row, n_col = lax.axis_size("row"), lax.axis_size("col")
    heads = memory_bias.shape[0]
    dims = Dims(n_row, n_col, heads, model_width // heads, row_dev, col_dev)
    me = lax.axis_index("row").astype(jnp.int32).reshape(1)
    args = (queries, keys, values)
    near_kgs, far_kgs = range(dims.head_groups // 2), range(dims.head_groups // 2, dims.head_groups)
    near = range(n_row // 2)
    far = range(n_row // 2, n_row)

    sent_far = list(spread(dims, far_kgs, me, args))
    me, sent_far[0] = lax.optimization_barrier((me, sent_far[0]))
    got_far = exchange(dims, far, sent_far)
    got_near = exchange(dims, near, spread(dims, near_kgs, me, args))

    pooled = pool(dims, keys, values)
    band = lax.all_gather(pooled[None], "col", axis=0, tiled=True)
    mem, lse = recall(dims, memory_bias, queries, band[:, 0], band[:, 1])

    blocks, mem, lse = lax.optimization_barrier((got_near + got_far, mem, lse))
    back_far = attend(dims, far, blocks)
    blocks, back_far = lax.optimization_barrier((blocks, back_far))
    home_far = exchange(dims, far, back_far)
    home_near = exchange(dims, near, attend(dims, near, blocks))
    out = collect(dims, near_kgs, me, mem, lse, home_near)
    return collect(dims, far_kgs, me, mem, lse, home_far, out)


def solution(mesh):
    return jax.shard_map(
        per_device,
        mesh=mesh,
        in_specs=(P("row", "col", None), P("row", "col", None), P("row", "col", None), P()),
        out_specs=P("row", "col", None),
        check_vma=False,
    )
```

```python
import functools
import math

import jax
import jax.numpy as jnp
from jax import lax
from jax.experimental import pallas as pl
from jax.experimental.pallas import tpu as pltpu
from jax.sharding import PartitionSpec as P


LOG2E = 1.4426950408889634
PARTS = 3
NT = (((1,), (1,)), ((), ()))
PARAMS = pltpu.CompilerParams(vmem_limit_bytes=20 * 1024 * 1024)
SMEM = pl.BlockSpec(memory_space=pltpu.SMEM)
VMEM = pl.BlockSpec(memory_space=pltpu.VMEM)
HBM = pl.BlockSpec(memory_space=pltpu.HBM)


def in_hbm(x):
    return pltpu.with_memory_space_constraint(x, pltpu.HBM)


class Dims:
    def __init__(self, n_row, n_col, heads, head_dim, row_dev, col_dev):
        self.n_row, self.n_col, self.head_dim = n_row, n_col, head_dim
        self.row_dev, self.col_dev, self.heads = row_dev, col_dev, heads
        self.head_groups = math.gcd(heads, n_row)
        self.col_groups = n_row // self.head_groups
        self.heads_g = heads // self.head_groups
        self.cols_g = col_dev // self.col_groups
        self.pairs = self.heads_g * self.cols_g
        self.width = self.heads_g * head_dim
        self.patches = row_dev * col_dev
        self.rows = n_row * row_dev
        self.sent_rows = 3 * self.pairs * row_dev
        self.folds = 2 if 2 * PARTS * self.pairs <= head_dim and row_dev % 32 == 0 else 1
        self.tail_rows = row_dev // self.folds
        self.back_rows = self.pairs * row_dev + self.tail_rows

    def lane(self, me, kg):
        return pl.multiple_of(((me // self.col_groups) ^ kg) * self.width, 128)

    def partners(self, kg):
        ks = range(kg * self.col_groups, (kg + 1) * self.col_groups)
        return sorted(ks, reverse=kg == 0)

    def at(self, k, pair):
        return (k * self.pairs + pair) * self.row_dev

    def column(self, me, kl, c):
        return ((me % self.col_groups) ^ kl) * self.cols_g + c


def spread_kernel(dims, kgs, me_ref, *refs):
    args, outs, (raw, wide, sems) = refs[:3], refs[3:-3], refs[-3:]
    me, head_dim, row_dev = me_ref[0], dims.head_dim, dims.row_dev
    loads = {}
    for i, kg in enumerate(kgs):
        for t, arg in enumerate(args):
            loads[i, t] = pltpu.make_async_copy(
                arg.at[:, :, pl.ds(dims.lane(me, kg), dims.width)], raw.at[i, t], sems.at[i, t]
            )
            loads[i, t].start()
    slot = 0
    for i in range(len(kgs)):
        for t in range(3):
            loads[i, t].wait()
            for j in range(dims.heads_g):
                wide[slot] = (
                    raw[i, t, :, :, j * head_dim : (j + 1) * head_dim]
                    .astype(jnp.float32)
                    .reshape(dims.patches, head_dim)
                )
                for n, k in enumerate(dims.partners(kgs[i])):
                    kl = k % dims.col_groups
                    for c in range(dims.cols_g):
                        at = (t * dims.pairs + j * dims.cols_g + c) * row_dev
                        outs[i * dims.col_groups + n][at : at + row_dev] = wide[
                            slot,
                            pl.ds(dims.column(me, kl, c), row_dev, stride=dims.col_dev),
                            :,
                        ].astype(jnp.bfloat16)
                slot = (slot + 1) % wide.shape[0]


def spread(dims, kgs, me, args):
    block = jax.ShapeDtypeStruct((dims.sent_rows, dims.head_dim), jnp.bfloat16)
    count = len(kgs) * dims.col_groups
    return pl.pallas_call(
        functools.partial(spread_kernel, dims, kgs),
        out_shape=[block] * count,
        in_specs=[SMEM] + [HBM] * 3,
        out_specs=[VMEM] * count,
        scratch_shapes=[
            pltpu.VMEM((len(kgs), 3, dims.row_dev, dims.col_dev, dims.width), jnp.bfloat16),
            pltpu.VMEM((4, dims.patches, dims.head_dim), jnp.float32),
            pltpu.SemaphoreType.DMA((len(kgs), 3)),
        ],
        compiler_params=PARAMS,
        name="spread",
    )(me, *[in_hbm(arg) for arg in args])


def pool_kernel(dims, k_ref, v_ref, out_ref, raw, sems):
    loads = [
        pltpu.make_async_copy(ref, raw.at[i], sems.at[i]) for i, ref in enumerate((k_ref, v_ref))
    ]
    for load in loads:
        load.start()
    for i, load in enumerate(loads):
        load.wait()
        total = jnp.zeros((dims.col_dev, raw.shape[-1]), jnp.float32)
        for r in range(dims.row_dev):
            total = total + raw[i, r].astype(jnp.float32)
        mean = jnp.sum(total, axis=0, keepdims=True) * (1.0 / dims.patches)
        out_ref[i : i + 1] = mean.astype(jnp.bfloat16).astype(jnp.float32)


def pool(dims, keys, values):
    return pl.pallas_call(
        functools.partial(pool_kernel, dims),
        out_shape=jax.ShapeDtypeStruct((2, keys.shape[-1]), jnp.float32),
        in_specs=[HBM] * 2,
        out_specs=VMEM,
        scratch_shapes=[
            pltpu.VMEM((2,) + keys.shape, jnp.bfloat16),
            pltpu.SemaphoreType.DMA((2,)),
        ],
        compiler_params=PARAMS,
        name="pool",
    )(in_hbm(keys), in_hbm(values)).astype(jnp.bfloat16)


def recall_kernel(
    dims, me_ref, bias_ref, q_ref, key_ref, value_ref, out_ref, lse_ref, raw, wide, wide_lse, sem
):
    load = pltpu.make_async_copy(q_ref, raw, sem)
    load.start()
    load.wait()
    me, head_dim, row_dev = me_ref[0], dims.head_dim, dims.row_dev
    scale = LOG2E / math.sqrt(head_dim)
    ones = jnp.ones((dims.n_col, head_dim), jnp.bfloat16)
    slot = 0
    for kg in range(dims.head_groups):
        lane = dims.lane(me, kg)
        for j in range(dims.heads_g):
            at = pl.ds(pl.multiple_of(lane + j * head_dim, 128), head_dim)
            query = raw[:, :, at].reshape(dims.patches, head_dim)
            key, value = key_ref[:, at], jnp.concatenate([value_ref[:, at], ones], axis=1)
            bias = bias_ref[((me // dims.col_groups) ^ kg) * dims.heads_g + j] * LOG2E
            score = lax.dot_general(query, key, NT, preferred_element_type=jnp.float32)
            score = score * scale + bias
            peak = jnp.max(score, axis=1, keepdims=True)
            weight = jnp.exp2(score - peak).astype(jnp.bfloat16)
            mixed = jnp.dot(weight, value, preferred_element_type=jnp.float32)
            total = mixed[:, head_dim:]
            wide[slot] = mixed[:, :head_dim] / total
            wide_lse[slot] = peak + jnp.log2(total)
            for kl in range(dims.col_groups):
                for c in range(dims.cols_g):
                    to = dims.at(kg * dims.col_groups + kl, j * dims.cols_g + c)
                    patch = pl.ds(dims.column(me, kl, c), row_dev, stride=dims.col_dev)
                    out_ref[to : to + row_dev] = wide[slot, patch, :]
                    lse_ref[to : to + row_dev] = wide_lse[slot, patch, :]
            slot = (slot + 1) % wide.shape[0]


def recall(dims, me, bias, queries, key, value):
    out = jax.ShapeDtypeStruct((dims.heads * dims.patches, dims.head_dim), jnp.float32)
    wide = pltpu.VMEM((4, dims.patches, dims.head_dim), jnp.float32)
    return pl.pallas_call(
        functools.partial(recall_kernel, dims),
        out_shape=[out] * 2,
        in_specs=[SMEM] * 2 + [HBM] + [VMEM] * 2,
        out_specs=[VMEM] * 2,
        scratch_shapes=[
            pltpu.VMEM(queries.shape, jnp.bfloat16),
            wide,
            wide,
            pltpu.SemaphoreType.DMA,
        ],
        compiler_params=PARAMS,
        name="recall",
    )(me, bias, in_hbm(queries), key, value)


def attend_kernel(dims, ks, *refs):
    ins, outs = refs[: dims.n_row], refs[dims.n_row :]
    row_dev, head_dim, rows = dims.row_dev, dims.head_dim, dims.rows
    count = len(ks) * row_dev
    scale = LOG2E / math.sqrt(head_dim)
    ones = jnp.ones((rows, head_dim), jnp.bfloat16)
    lane = lax.broadcasted_iota(jnp.int32, (count, head_dim), 1)
    row = lax.broadcasted_iota(jnp.int32, (count, head_dim), 0) % row_dev
    lane = lane - row // dims.tail_rows * (head_dim // dims.folds)
    tail = jnp.zeros((count, head_dim), jnp.float32)

    def gather(t, pair, sources):
        at = (t * dims.pairs + pair) * row_dev
        return jnp.concatenate([ins[k][at : at + row_dev] for k in sources], axis=0)

    for pair in range(dims.pairs):
        query = gather(0, pair, ks)
        key = gather(1, pair, range(dims.n_row))
        value = jnp.concatenate([gather(2, pair, range(dims.n_row)), ones], axis=1)
        score = lax.dot_general(query, key, NT, preferred_element_type=jnp.float32) * scale
        peak = jnp.max(score, axis=1, keepdims=True)
        weight = jnp.exp2(score - peak).astype(jnp.bfloat16)
        mixed = jnp.dot(weight, value, preferred_element_type=jnp.float32)
        total = mixed[:, head_dim:]
        out = (mixed[:, :head_dim] / total).astype(jnp.bfloat16)
        rest = peak + jnp.log2(total)
        for part in range(PARTS):
            term = rest.astype(jnp.bfloat16).astype(jnp.float32)
            tail = jnp.where(lane == pair * PARTS + part, term, tail)
            rest = rest - term
        for i in range(len(ks)):
            outs[i][pair * row_dev : (pair + 1) * row_dev] = out[i * row_dev : (i + 1) * row_dev]
    for i in range(len(ks)):
        folded = jnp.zeros((dims.tail_rows, head_dim), jnp.float32)
        for fold in range(dims.folds):
            at = i * row_dev + fold * dims.tail_rows
            folded = folded + tail[at : at + dims.tail_rows]
        outs[i][dims.pairs * row_dev :] = folded.astype(jnp.bfloat16)


def attend(dims, ks, blocks):
    block = jax.ShapeDtypeStruct((dims.back_rows, dims.head_dim), jnp.bfloat16)
    return pl.pallas_call(
        functools.partial(attend_kernel, dims, ks),
        out_shape=[block] * len(ks),
        in_specs=[VMEM] * dims.n_row,
        out_specs=[VMEM] * len(ks),
        compiler_params=PARAMS,
        name="attend",
    )(*blocks)


def collect_kernel(dims, kgs, me_ref, mem_ref, lse_ref, *refs):
    blocks = refs[: len(kgs) * dims.col_groups]
    out, wide, done, sems = refs[-4:]
    me, head_dim, row_dev = me_ref[0], dims.head_dim, dims.row_dev
    shape = (head_dim, dims.pairs * head_dim)
    row = lax.broadcasted_iota(jnp.int32, shape, 0)
    pair_of = lax.broadcasted_iota(jnp.int32, shape, 1) // head_dim
    stores = []
    slot = 0
    for i, kg in enumerate(kgs):
        mine = blocks[i * dims.col_groups : (i + 1) * dims.col_groups]
        tails = jnp.concatenate([ref[dims.pairs * row_dev :] for ref in mine], axis=0)
        lses = []
        for fold in range(dims.folds):
            first = fold * (head_dim // dims.folds)
            pick = ((row >= first) & ((row - first) // PARTS == pair_of)).astype(jnp.bfloat16)
            lses.append(jnp.dot(tails, pick, preferred_element_type=jnp.float32))
        lane = dims.lane(me, kg)
        for j in range(dims.heads_g):
            for n, ref in enumerate(mine):
                kl = dims.partners(kg)[n] % dims.col_groups
                for c in range(dims.cols_g):
                    pair = j * dims.cols_g + c
                    lanes = slice(pair * head_dim, (pair + 1) * head_dim)
                    rows = slice(n * dims.tail_rows, (n + 1) * dims.tail_rows)
                    lse = jnp.concatenate([part[rows, lanes] for part in lses], axis=0)
                    at = dims.at(kg * dims.col_groups + kl, pair)
                    mem = mem_ref[at : at + row_dev]
                    share = 1.0 / (1.0 + jnp.exp2(lse_ref[at : at + row_dev] - lse))
                    col = ref[pair * row_dev : (pair + 1) * row_dev].astype(jnp.float32)
                    to = pl.ds(dims.column(me, kl, c), row_dev, stride=dims.col_dev)
                    wide[slot, to, :] = mem + share * (col - mem)
            done[i, j] = (
                wide[slot].astype(jnp.bfloat16).reshape(row_dev, dims.col_dev, head_dim)
            )
            at = pl.ds(pl.multiple_of(lane + j * head_dim, 128), head_dim)
            stores.append(
                pltpu.make_async_copy(done.at[i, j], out.at[:, :, at], sems.at[i, j])
            )
            stores[-1].start()
            slot = (slot + 1) % wide.shape[0]
    for store in stores:
        store.wait()


def collect(dims, kgs, me, mem, lse, blocks, out=None):
    shape = (dims.row_dev, dims.col_dev, dims.heads * dims.head_dim)
    operands = (me, mem, lse, *blocks) + (() if out is None else (out,))
    return pl.pallas_call(
        functools.partial(collect_kernel, dims, kgs),
        out_shape=jax.ShapeDtypeStruct(shape, jnp.bfloat16),
        in_specs=[SMEM] + [VMEM] * (2 + len(blocks)) + [HBM] * (out is not None),
        out_specs=HBM,
        scratch_shapes=[
            pltpu.VMEM((4, dims.patches, dims.head_dim), jnp.float32),
            pltpu.VMEM((len(kgs), dims.heads_g) + shape[:2] + (dims.head_dim,), jnp.bfloat16),
            pltpu.SemaphoreType.DMA((len(kgs), dims.heads_g)),
        ],
        input_output_aliases={} if out is None else {len(operands) - 1: 0},
        compiler_params=PARAMS,
        name="collect",
    )(*operands)


def exchange(dims, ks, blocks):
    return [
        lax.ppermute(block, "row", [(i, i ^ k) for i in range(dims.n_row)]) if k else block
        for k, block in zip(ks, blocks)
    ]


def per_device(queries, keys, values, memory_bias):
    row_dev, col_dev, model_width = queries.shape
    n_row, n_col = lax.axis_size("row"), lax.axis_size("col")
    heads = memory_bias.shape[0]
    dims = Dims(n_row, n_col, heads, model_width // heads, row_dev, col_dev)
    me = lax.axis_index("row").astype(jnp.int32).reshape(1)
    args = (queries, keys, values)
    order = (*range(1, dims.head_groups), 0)
    flat = [k for kg in order for k in dims.partners(kg)]
    lead = dims.head_groups // 2
    waves = [kgs for kgs in ((lead,), tuple(kg for kg in order if kg != lead)) if kgs]

    got, token = {}, me
    for kgs in waves:
        ks = [k for kg in kgs for k in dims.partners(kg)]
        sent = list(spread(dims, kgs, token, args))
        got.update(zip(ks, exchange(dims, ks, sent)))
        token, _ = lax.optimization_barrier((me, sent[0]))

    pooled = pool(dims, keys, values)
    band = lax.all_gather(pooled[None], "col", axis=0, tiled=True)
    mem, lse = recall(dims, me, memory_bias, queries, band[:, 0], band[:, 1])

    got, mem, lse = lax.optimization_barrier(([got[k] for k in flat], mem, lse))
    home = {}
    for kgs in waves:
        ks = [k for kg in kgs for k in dims.partners(kg)]
        back = attend(dims, ks, [got[flat.index(k)] for k in range(n_row)])
        got, back = lax.optimization_barrier((got, list(back)))
        home.update(zip(ks, exchange(dims, ks, back)))
    return collect(dims, order, me, mem, lse, [home[k] for k in flat])


def solution(mesh):
    return jax.shard_map(
        per_device,
        mesh=mesh,
        in_specs=(P("row", "col", None), P("row", "col", None), P("row", "col", None), P()),
        out_specs=P("row", "col", None),
        check_vma=False,
    )
```

```python
import functools
import math

import jax
import jax.numpy as jnp
from jax import lax
from jax.experimental import pallas as pl
from jax.experimental.pallas import tpu as pltpu
from jax.sharding import PartitionSpec as P


LOG2E = 1.4426950408889634
PARTS = 3
NT = (((1,), (1,)), ((), ()))
PARAMS = pltpu.CompilerParams(vmem_limit_bytes=20 * 1024 * 1024)
SMEM = pl.BlockSpec(memory_space=pltpu.SMEM)
VMEM = pl.BlockSpec(memory_space=pltpu.VMEM)
HBM = pl.BlockSpec(memory_space=pltpu.HBM)


def in_hbm(x):
    return pltpu.with_memory_space_constraint(x, pltpu.HBM)


class Dims:
    def __init__(self, n_row, n_col, heads, head_dim, row_dev, col_dev):
        self.n_row, self.n_col, self.head_dim = n_row, n_col, head_dim
        self.row_dev, self.col_dev, self.heads = row_dev, col_dev, heads
        self.head_groups = math.gcd(heads, n_row)
        self.col_groups = n_row // self.head_groups
        self.heads_g = heads // self.head_groups
        self.cols_g = col_dev // self.col_groups
        self.pairs = self.heads_g * self.cols_g
        self.width = self.heads_g * head_dim
        self.patches = row_dev * col_dev
        self.rows = n_row * row_dev
        self.sent_rows = 3 * self.pairs * row_dev
        self.folds = 2 if 2 * PARTS * self.pairs <= head_dim and row_dev % 32 == 0 else 1
        self.tail_rows = row_dev // self.folds
        self.back_rows = self.pairs * row_dev + self.tail_rows

    def lane(self, me, kg):
        return pl.multiple_of(((me // self.col_groups) ^ kg) * self.width, 128)

    def fold_lanes(self, lane, row_dev):
        row = lax.broadcasted_iota(jnp.int32, lane.shape, 0) % row_dev
        return lane - row // self.tail_rows * (self.head_dim // self.folds)

    def fold(self, tail):
        parts = [
            tail[i * self.tail_rows : (i + 1) * self.tail_rows] for i in range(self.folds)
        ]
        return functools.reduce(lambda a, b: a + b, parts)

    def partners(self, kg):
        ks = range(kg * self.col_groups, (kg + 1) * self.col_groups)
        return sorted(ks, reverse=kg == 0)

    def at(self, k, pair):
        return (k * self.pairs + pair) * self.row_dev

    def column(self, me, kl, c):
        return ((me % self.col_groups) ^ kl) * self.cols_g + c


def spread_kernel(dims, kgs, me_ref, *refs):
    args, outs, (raw, wide, sems) = refs[:3], refs[3:-3], refs[-3:]
    me, head_dim, row_dev = me_ref[0], dims.head_dim, dims.row_dev
    loads = {}
    for i, kg in enumerate(kgs):
        for t, arg in enumerate(args):
            loads[i, t] = pltpu.make_async_copy(
                arg.at[:, :, pl.ds(dims.lane(me, kg), dims.width)], raw.at[i, t], sems.at[i, t]
            )
            loads[i, t].start()
    slot = 0
    for i in range(len(kgs)):
        for t in range(3):
            loads[i, t].wait()
            for j in range(dims.heads_g):
                wide[slot] = (
                    raw[i, t, :, :, j * head_dim : (j + 1) * head_dim]
                    .astype(jnp.float32)
                    .reshape(dims.patches, head_dim)
                )
                for n, k in enumerate(dims.partners(kgs[i])):
                    kl = k % dims.col_groups
                    for c in range(dims.cols_g):
                        at = (t * dims.pairs + j * dims.cols_g + c) * row_dev
                        outs[i * dims.col_groups + n][at : at + row_dev] = wide[
                            slot,
                            pl.ds(dims.column(me, kl, c), row_dev, stride=dims.col_dev),
                            :,
                        ].astype(jnp.bfloat16)
                slot = (slot + 1) % wide.shape[0]


def spread(dims, kgs, me, args):
    block = jax.ShapeDtypeStruct((dims.sent_rows, dims.head_dim), jnp.bfloat16)
    count = len(kgs) * dims.col_groups
    return pl.pallas_call(
        functools.partial(spread_kernel, dims, kgs),
        out_shape=[block] * count,
        in_specs=[SMEM] + [HBM] * 3,
        out_specs=[VMEM] * count,
        scratch_shapes=[
            pltpu.VMEM((len(kgs), 3, dims.row_dev, dims.col_dev, dims.width), jnp.bfloat16),
            pltpu.VMEM((4, dims.patches, dims.head_dim), jnp.float32),
            pltpu.SemaphoreType.DMA((len(kgs), 3)),
        ],
        compiler_params=PARAMS,
        name="spread",
    )(me, *[in_hbm(arg) for arg in args])


def pool_kernel(dims, k_ref, v_ref, out_ref, raw, sems):
    loads = [
        pltpu.make_async_copy(ref, raw.at[i], sems.at[i]) for i, ref in enumerate((k_ref, v_ref))
    ]
    for load in loads:
        load.start()
    for i, load in enumerate(loads):
        load.wait()
        total = jnp.zeros((dims.col_dev, raw.shape[-1]), jnp.float32)
        for r in range(dims.row_dev):
            total = total + raw[i, r].astype(jnp.float32)
        mean = jnp.sum(total, axis=0, keepdims=True) * (1.0 / dims.patches)
        out_ref[i : i + 1] = mean.astype(jnp.bfloat16).astype(jnp.float32)


def pool(dims, keys, values):
    return pl.pallas_call(
        functools.partial(pool_kernel, dims),
        out_shape=jax.ShapeDtypeStruct((2, keys.shape[-1]), jnp.float32),
        in_specs=[HBM] * 2,
        out_specs=VMEM,
        scratch_shapes=[
            pltpu.VMEM((2,) + keys.shape, jnp.bfloat16),
            pltpu.SemaphoreType.DMA((2,)),
        ],
        compiler_params=PARAMS,
        name="pool",
    )(in_hbm(keys), in_hbm(values)).astype(jnp.bfloat16)


def recall_kernel(
    dims, me_ref, bias_ref, q_ref, key_ref, value_ref, out_ref, lse_ref, raw, wide, wide_lse, sem
):
    load = pltpu.make_async_copy(q_ref, raw, sem)
    load.start()
    load.wait()
    me, head_dim, row_dev = me_ref[0], dims.head_dim, dims.row_dev
    scale = LOG2E / math.sqrt(head_dim)
    ones = jnp.ones((dims.n_col, head_dim), jnp.bfloat16)
    column = dims.fold_lanes(lax.broadcasted_iota(jnp.int32, (row_dev, head_dim), 1), row_dev)
    slot = 0
    for kg in range(dims.head_groups):
        lane = dims.lane(me, kg)
        tails = [jnp.zeros((row_dev, head_dim), jnp.float32)] * dims.col_groups
        for j in range(dims.heads_g):
            at = pl.ds(pl.multiple_of(lane + j * head_dim, 128), head_dim)
            query = raw[:, :, at].reshape(dims.patches, head_dim)
            key, value = key_ref[:, at], jnp.concatenate([value_ref[:, at], ones], axis=1)
            bias = bias_ref[((me // dims.col_groups) ^ kg) * dims.heads_g + j] * LOG2E
            score = lax.dot_general(query, key, NT, preferred_element_type=jnp.float32)
            score = score * scale + bias
            peak = jnp.max(score, axis=1, keepdims=True)
            weight = jnp.exp2(score - peak).astype(jnp.bfloat16)
            mixed = jnp.dot(weight, value, preferred_element_type=jnp.float32)
            total = mixed[:, head_dim:]
            wide[slot] = mixed[:, :head_dim] / total
            wide_lse[slot] = peak + jnp.log2(total)
            for kl in range(dims.col_groups):
                for c in range(dims.cols_g):
                    to = dims.at(kg * dims.col_groups + kl, j * dims.cols_g + c)
                    patch = pl.ds(dims.column(me, kl, c), row_dev, stride=dims.col_dev)
                    out_ref[to : to + row_dev] = wide[slot, patch, :]
                    pair = j * dims.cols_g + c
                    tails[kl] = jnp.where(column == pair, wide_lse[slot, patch, :], tails[kl])
            slot = (slot + 1) % wide.shape[0]
        for kl, tail in enumerate(tails):
            to = (kg * dims.col_groups + kl) * dims.tail_rows
            lse_ref[to : to + dims.tail_rows] = dims.fold(tail)


def recall(dims, me, bias, queries, key, value):
    out = jax.ShapeDtypeStruct((dims.heads * dims.patches, dims.head_dim), jnp.float32)
    tails = jax.ShapeDtypeStruct((dims.n_row * dims.tail_rows, dims.head_dim), jnp.float32)
    wide = pltpu.VMEM((4, dims.patches, dims.head_dim), jnp.float32)
    return pl.pallas_call(
        functools.partial(recall_kernel, dims),
        out_shape=[out, tails],
        in_specs=[SMEM] * 2 + [HBM] + [VMEM] * 2,
        out_specs=[VMEM] * 2,
        scratch_shapes=[
            pltpu.VMEM(queries.shape, jnp.bfloat16),
            wide,
            wide,
            pltpu.SemaphoreType.DMA,
        ],
        compiler_params=PARAMS,
        name="recall",
    )(me, bias, in_hbm(queries), key, value)


def attend_kernel(dims, ks, *refs):
    ins, outs = refs[: dims.n_row], refs[dims.n_row :]
    row_dev, head_dim, rows = dims.row_dev, dims.head_dim, dims.rows
    count = len(ks) * row_dev
    scale = LOG2E / math.sqrt(head_dim)
    ones = jnp.ones((rows, head_dim), jnp.bfloat16)
    lane = dims.fold_lanes(lax.broadcasted_iota(jnp.int32, (count, head_dim), 1), row_dev)
    tail = jnp.zeros((count, head_dim), jnp.float32)

    def gather(t, pair, sources):
        at = (t * dims.pairs + pair) * row_dev
        return jnp.concatenate([ins[k][at : at + row_dev] for k in sources], axis=0)

    for pair in range(dims.pairs):
        query = gather(0, pair, ks)
        key = gather(1, pair, range(dims.n_row))
        value = jnp.concatenate([gather(2, pair, range(dims.n_row)), ones], axis=1)
        score = lax.dot_general(query, key, NT, preferred_element_type=jnp.float32) * scale
        peak = jnp.max(score, axis=1, keepdims=True)
        weight = jnp.exp2(score - peak).astype(jnp.bfloat16)
        mixed = jnp.dot(weight, value, preferred_element_type=jnp.float32)
        total = mixed[:, head_dim:]
        out = (mixed[:, :head_dim] / total).astype(jnp.bfloat16)
        rest = peak + jnp.log2(total)
        for part in range(PARTS):
            term = rest.astype(jnp.bfloat16).astype(jnp.float32)
            tail = jnp.where(lane == pair * PARTS + part, term, tail)
            rest = rest - term
        for i in range(len(ks)):
            outs[i][pair * row_dev : (pair + 1) * row_dev] = out[i * row_dev : (i + 1) * row_dev]
    for i in range(len(ks)):
        folded = dims.fold(tail[i * row_dev : (i + 1) * row_dev])
        outs[i][dims.pairs * row_dev :] = folded.astype(jnp.bfloat16)


def attend(dims, ks, blocks):
    block = jax.ShapeDtypeStruct((dims.back_rows, dims.head_dim), jnp.bfloat16)
    return pl.pallas_call(
        functools.partial(attend_kernel, dims, ks),
        out_shape=[block] * len(ks),
        in_specs=[VMEM] * dims.n_row,
        out_specs=[VMEM] * len(ks),
        compiler_params=PARAMS,
        name="attend",
    )(*blocks)


def collect_kernel(dims, kgs, me_ref, mem_ref, lse_ref, *refs):
    ks = [k for kg in kgs for k in dims.partners(kg)]
    blocks = dict(zip(ks, refs))
    out, wide, done, sems = refs[-4:]
    me, head_dim, row_dev, size = me_ref[0], dims.head_dim, dims.row_dev, dims.tail_rows
    span = head_dim // dims.folds

    def one_hot(shape, match):
        row = lax.broadcasted_iota(jnp.int32, shape, 0) % head_dim
        return match(row, lax.broadcasted_iota(jnp.int32, shape, 1)).astype(jnp.bfloat16)

    tails = jnp.concatenate([blocks[k][dims.pairs * row_dev :] for k in ks], axis=0)
    join = one_hot(
        (head_dim, head_dim),
        lambda row, col: (row // span == col // span) & (row % span // PARTS == col % span),
    )
    col_lse = jnp.dot(tails, join, preferred_element_type=jnp.float32)
    mem_lse = jnp.concatenate([lse_ref[k * size : (k + 1) * size] for k in ks], axis=0)
    share = 1.0 / (1.0 + jnp.exp2(mem_lse - col_lse))
    high = share.astype(jnp.bfloat16)
    low = (share - high.astype(jnp.float32)).astype(jnp.bfloat16)
    terms = jnp.concatenate([high, low], axis=1)
    shares = []
    for fold in range(dims.folds):
        pick = one_hot(
            (2 * head_dim, dims.pairs * head_dim),
            lambda row, col: row - fold * span == col // head_dim,
        )
        shares.append(jnp.dot(terms, pick, preferred_element_type=jnp.float32))

    stores = []
    slot = 0
    for i, kg in enumerate(kgs):
        lane = dims.lane(me, kg)
        for j in range(dims.heads_g):
            for k in dims.partners(kg):
                for c in range(dims.cols_g):
                    pair = j * dims.cols_g + c
                    lanes = slice(pair * head_dim, (pair + 1) * head_dim)
                    rows = slice(ks.index(k) * size, (ks.index(k) + 1) * size)
                    part = jnp.concatenate([fold[rows, lanes] for fold in shares], axis=0)
                    at = dims.at(k, pair)
                    mem = mem_ref[at : at + row_dev]
                    col = blocks[k][pair * row_dev : (pair + 1) * row_dev].astype(jnp.float32)
                    to = pl.ds(
                        dims.column(me, k % dims.col_groups, c), row_dev, stride=dims.col_dev
                    )
                    wide[slot, to, :] = mem + part * (col - mem)
            done[i, j] = (
                wide[slot].astype(jnp.bfloat16).reshape(row_dev, dims.col_dev, head_dim)
            )
            at = pl.ds(pl.multiple_of(lane + j * head_dim, 128), head_dim)
            stores.append(
                pltpu.make_async_copy(done.at[i, j], out.at[:, :, at], sems.at[i, j])
            )
            stores[-1].start()
            slot = (slot + 1) % wide.shape[0]
    for store in stores:
        store.wait()


def collect(dims, kgs, me, mem, lse, blocks, out=None):
    shape = (dims.row_dev, dims.col_dev, dims.heads * dims.head_dim)
    operands = (me, mem, lse, *blocks) + (() if out is None else (out,))
    return pl.pallas_call(
        functools.partial(collect_kernel, dims, kgs),
        out_shape=jax.ShapeDtypeStruct(shape, jnp.bfloat16),
        in_specs=[SMEM] + [VMEM] * (2 + len(blocks)) + [HBM] * (out is not None),
        out_specs=HBM,
        scratch_shapes=[
            pltpu.VMEM((4, dims.patches, dims.head_dim), jnp.float32),
            pltpu.VMEM((len(kgs), dims.heads_g) + shape[:2] + (dims.head_dim,), jnp.bfloat16),
            pltpu.SemaphoreType.DMA((len(kgs), dims.heads_g)),
        ],
        input_output_aliases={} if out is None else {len(operands) - 1: 0},
        compiler_params=PARAMS,
        name="collect",
    )(*operands)


def exchange(dims, ks, blocks):
    return [
        lax.ppermute(block, "row", [(i, i ^ k) for i in range(dims.n_row)]) if k else block
        for k, block in zip(ks, blocks)
    ]


def per_device(queries, keys, values, memory_bias):
    row_dev, col_dev, model_width = queries.shape
    n_row, n_col = lax.axis_size("row"), lax.axis_size("col")
    heads = memory_bias.shape[0]
    dims = Dims(n_row, n_col, heads, model_width // heads, row_dev, col_dev)
    me = lax.axis_index("row").astype(jnp.int32).reshape(1)
    args = (queries, keys, values)
    order = (*range(1, dims.head_groups), 0)
    flat = [k for kg in order for k in dims.partners(kg)]
    lead = dims.head_groups // 2
    waves = [kgs for kgs in ((lead,), tuple(kg for kg in order if kg != lead)) if kgs]

    back_waves = [(lead, 0), tuple(kg for kg in order if kg not in (lead, 0))] if lead else [order]

    got, token = {}, me
    for kgs in waves:
        ks = [k for kg in kgs for k in dims.partners(kg)]
        sent = list(spread(dims, kgs, token, args))
        got.update(zip(ks, exchange(dims, ks, sent)))
        token, _ = lax.optimization_barrier((me, sent[0]))

    pooled = pool(dims, keys, values)
    band = lax.all_gather(pooled[None], "col", axis=0, tiled=True)
    mem, lse = recall(dims, me, memory_bias, queries, band[:, 0], band[:, 1])

    got, mem, lse = lax.optimization_barrier(([got[k] for k in flat], mem, lse))
    home = {}
    for kgs in back_waves:
        ks = [k for kg in kgs for k in dims.partners(kg)]
        back = attend(dims, ks, [got[flat.index(k)] for k in range(n_row)])
        got, back = lax.optimization_barrier((got, list(back)))
        home.update(zip(ks, exchange(dims, ks, back)))
    out = None
    for kgs in [(0, lead), back_waves[1]] if lead else [order]:
        ks = [k for kg in kgs for k in dims.partners(kg)]
        out = collect(dims, kgs, me, mem, lse, [home[k] for k in ks], out)
    return out


def solution(mesh):
    return jax.shard_map(
        per_device,
        mesh=mesh,
        in_specs=(P("row", "col", None), P("row", "col", None), P("row", "col", None), P()),
        out_specs=P("row", "col", None),
        check_vma=False,
    )
```

```python
import functools
import math

import jax
import jax.numpy as jnp
from jax import lax
from jax.experimental import pallas as pl
from jax.experimental.pallas import tpu as pltpu
from jax.sharding import PartitionSpec as P


LOG2E = 1.4426950408889634
PARTS = 3
NT = (((1,), (1,)), ((), ()))
PARAMS = pltpu.CompilerParams(vmem_limit_bytes=20 * 1024 * 1024)
SMEM = pl.BlockSpec(memory_space=pltpu.SMEM)
VMEM = pl.BlockSpec(memory_space=pltpu.VMEM)
HBM = pl.BlockSpec(memory_space=pltpu.HBM)


def in_hbm(x):
    return pltpu.with_memory_space_constraint(x, pltpu.HBM)


class Dims:
    def __init__(self, n_row, n_col, heads, head_dim, row_dev, col_dev):
        self.n_row, self.n_col, self.head_dim = n_row, n_col, head_dim
        self.row_dev, self.col_dev, self.heads = row_dev, col_dev, heads
        self.head_groups = math.gcd(heads, n_row)
        self.col_groups = n_row // self.head_groups
        self.heads_g = heads // self.head_groups
        self.cols_g = col_dev // self.col_groups
        self.pairs = self.heads_g * self.cols_g
        self.width = self.heads_g * head_dim
        self.patches = row_dev * col_dev
        self.rows = n_row * row_dev
        self.folds = 2 if 2 * PARTS * self.pairs <= head_dim and row_dev % 32 == 0 else 1
        self.tail_rows = row_dev // self.folds
        self.back_rows = self.pairs * row_dev + self.tail_rows

    def lane(self, me, kg):
        return pl.multiple_of(((me // self.col_groups) ^ kg) * self.width, 128)

    def fold_lanes(self, lane, row_dev):
        row = lax.broadcasted_iota(jnp.int32, lane.shape, 0) % row_dev
        return lane - row // self.tail_rows * (self.head_dim // self.folds)

    def fold(self, tail):
        parts = [
            tail[i * self.tail_rows : (i + 1) * self.tail_rows] for i in range(self.folds)
        ]
        return functools.reduce(lambda a, b: a + b, parts)

    def pieces(self, k):
        return ((1, 2), (0,)) if k >= self.n_row - self.col_groups else ((0, 1, 2),)

    def row(self, kinds, kind, pair):
        return (kinds.index(kind) * self.pairs + pair) * self.row_dev

    def partners(self, kg):
        ks = range(kg * self.col_groups, (kg + 1) * self.col_groups)
        return sorted(ks, reverse=kg == 0)

    def at(self, k, pair):
        return (k * self.pairs + pair) * self.row_dev

    def column(self, me, kl, c):
        return ((me % self.col_groups) ^ kl) * self.cols_g + c


def spread_kernel(dims, parts, me_ref, *refs):
    args, outs, raws, (wide, sems) = (
        refs[:3],
        refs[3 : -2 - len(parts)],
        refs[-2 - len(parts) : -2],
        refs[-2:],
    )
    me, head_dim, row_dev = me_ref[0], dims.head_dim, dims.row_dev
    loads = {}
    for i, (kg, kinds) in enumerate(parts):
        for n, kind in enumerate(kinds):
            loads[i, n] = pltpu.make_async_copy(
                args[kind].at[:, :, pl.ds(dims.lane(me, kg), dims.width)],
                raws[i].at[n],
                sems.at[i, n],
            )
            loads[i, n].start()
    slot = 0
    for i, (kg, kinds) in enumerate(parts):
        ks = dims.partners(kg)
        mine, outs = outs[: len(ks)], outs[len(ks) :]
        for n, kind in enumerate(kinds):
            loads[i, n].wait()
            for j in range(dims.heads_g):
                wide[slot] = (
                    raws[i][n, :, :, j * head_dim : (j + 1) * head_dim]
                    .astype(jnp.float32)
                    .reshape(dims.patches, head_dim)
                )
                for k, out in zip(ks, mine):
                    for c in range(dims.cols_g):
                        patch = pl.ds(
                            dims.column(me, k % dims.col_groups, c), row_dev, stride=dims.col_dev
                        )
                        at = dims.row(kinds, kind, j * dims.cols_g + c)
                        out[at : at + row_dev] = wide[slot, patch, :].astype(jnp.bfloat16)
                slot = (slot + 1) % wide.shape[0]


def spread(dims, parts, me, args):
    keys = [(k, kinds) for kg, kinds in parts for k in dims.partners(kg)]
    rows = dims.pairs * dims.row_dev
    blocks = pl.pallas_call(
        functools.partial(spread_kernel, dims, parts),
        out_shape=[
            jax.ShapeDtypeStruct((len(kinds) * rows, dims.head_dim), jnp.bfloat16)
            for _, kinds in keys
        ],
        in_specs=[SMEM] + [HBM] * 3,
        out_specs=[VMEM] * len(keys),
        scratch_shapes=[
            pltpu.VMEM((len(kinds), dims.row_dev, dims.col_dev, dims.width), jnp.bfloat16)
            for _, kinds in parts
        ]
        + [
            pltpu.VMEM((4, dims.patches, dims.head_dim), jnp.float32),
            pltpu.SemaphoreType.DMA((len(parts), 3)),
        ],
        compiler_params=PARAMS,
        name="spread",
    )(me, *[in_hbm(arg) for arg in args])
    return dict(zip(keys, blocks))


def pool_kernel(dims, k_ref, v_ref, out_ref, raw, sems):
    loads = [
        pltpu.make_async_copy(ref, raw.at[i], sems.at[i]) for i, ref in enumerate((k_ref, v_ref))
    ]
    for load in loads:
        load.start()
    for i, load in enumerate(loads):
        load.wait()
        total = jnp.zeros((dims.col_dev, raw.shape[-1]), jnp.float32)
        for r in range(dims.row_dev):
            total = total + raw[i, r].astype(jnp.float32)
        mean = jnp.sum(total, axis=0, keepdims=True) * (1.0 / dims.patches)
        out_ref[i : i + 1] = mean.astype(jnp.bfloat16).astype(jnp.float32)


def pool(dims, keys, values):
    return pl.pallas_call(
        functools.partial(pool_kernel, dims),
        out_shape=jax.ShapeDtypeStruct((2, keys.shape[-1]), jnp.float32),
        in_specs=[HBM] * 2,
        out_specs=VMEM,
        scratch_shapes=[
            pltpu.VMEM((2,) + keys.shape, jnp.bfloat16),
            pltpu.SemaphoreType.DMA((2,)),
        ],
        compiler_params=PARAMS,
        name="pool",
    )(in_hbm(keys), in_hbm(values)).astype(jnp.bfloat16)


def recall_kernel(
    dims, me_ref, bias_ref, q_ref, key_ref, value_ref, out_ref, lse_ref, raw, wide, wide_lse, sem
):
    load = pltpu.make_async_copy(q_ref, raw, sem)
    load.start()
    load.wait()
    me, head_dim, row_dev = me_ref[0], dims.head_dim, dims.row_dev
    scale = LOG2E / math.sqrt(head_dim)
    ones = jnp.ones((dims.n_col, head_dim), jnp.bfloat16)
    column = dims.fold_lanes(lax.broadcasted_iota(jnp.int32, (row_dev, head_dim), 1), row_dev)
    slot = 0
    for kg in range(dims.head_groups):
        lane = dims.lane(me, kg)
        tails = [jnp.zeros((row_dev, head_dim), jnp.float32)] * dims.col_groups
        for j in range(dims.heads_g):
            at = pl.ds(pl.multiple_of(lane + j * head_dim, 128), head_dim)
            query = raw[:, :, at].reshape(dims.patches, head_dim)
            key, value = key_ref[:, at], jnp.concatenate([value_ref[:, at], ones], axis=1)
            bias = bias_ref[((me // dims.col_groups) ^ kg) * dims.heads_g + j] * LOG2E
            score = lax.dot_general(query, key, NT, preferred_element_type=jnp.float32)
            score = score * scale + bias
            peak = jnp.max(score, axis=1, keepdims=True)
            weight = jnp.exp2(score - peak).astype(jnp.bfloat16)
            mixed = jnp.dot(weight, value, preferred_element_type=jnp.float32)
            total = mixed[:, head_dim:]
            wide[slot] = mixed[:, :head_dim] / total
            wide_lse[slot] = peak + jnp.log2(total)
            for kl in range(dims.col_groups):
                for c in range(dims.cols_g):
                    to = dims.at(kg * dims.col_groups + kl, j * dims.cols_g + c)
                    patch = pl.ds(dims.column(me, kl, c), row_dev, stride=dims.col_dev)
                    out_ref[to : to + row_dev] = wide[slot, patch, :]
                    pair = j * dims.cols_g + c
                    tails[kl] = jnp.where(column == pair, wide_lse[slot, patch, :], tails[kl])
            slot = (slot + 1) % wide.shape[0]
        for kl, tail in enumerate(tails):
            to = (kg * dims.col_groups + kl) * dims.tail_rows
            lse_ref[to : to + dims.tail_rows] = dims.fold(tail)


def recall(dims, me, bias, queries, key, value):
    out = jax.ShapeDtypeStruct((dims.heads * dims.patches, dims.head_dim), jnp.float32)
    tails = jax.ShapeDtypeStruct((dims.n_row * dims.tail_rows, dims.head_dim), jnp.float32)
    wide = pltpu.VMEM((4, dims.patches, dims.head_dim), jnp.float32)
    return pl.pallas_call(
        functools.partial(recall_kernel, dims),
        out_shape=[out, tails],
        in_specs=[SMEM] * 2 + [HBM] + [VMEM] * 2,
        out_specs=[VMEM] * 2,
        scratch_shapes=[
            pltpu.VMEM(queries.shape, jnp.bfloat16),
            wide,
            wide,
            pltpu.SemaphoreType.DMA,
        ],
        compiler_params=PARAMS,
        name="recall",
    )(me, bias, in_hbm(queries), key, value)


def attend_kernel(dims, ks, keys, *refs):
    ins, outs = dict(zip(keys, refs)), refs[len(keys) :]
    row_dev, head_dim, rows = dims.row_dev, dims.head_dim, dims.rows
    count = len(ks) * row_dev
    scale = LOG2E / math.sqrt(head_dim)
    ones = jnp.ones((rows, head_dim), jnp.bfloat16)
    lane = dims.fold_lanes(lax.broadcasted_iota(jnp.int32, (count, head_dim), 1), row_dev)
    tail = jnp.zeros((count, head_dim), jnp.float32)

    def gather(kind, pair, sources):
        parts = []
        for k in sources:
            kinds = [piece for piece in dims.pieces(k) if kind in piece][0]
            at = dims.row(kinds, kind, pair)
            parts.append(ins[k, kinds][at : at + row_dev])
        return jnp.concatenate(parts, axis=0)

    for pair in range(dims.pairs):
        query = gather(0, pair, ks)
        key = gather(1, pair, range(dims.n_row))
        value = jnp.concatenate([gather(2, pair, range(dims.n_row)), ones], axis=1)
        score = lax.dot_general(query, key, NT, preferred_element_type=jnp.float32) * scale
        peak = jnp.max(score, axis=1, keepdims=True)
        weight = jnp.exp2(score - peak).astype(jnp.bfloat16)
        mixed = jnp.dot(weight, value, preferred_element_type=jnp.float32)
        total = mixed[:, head_dim:]
        out = (mixed[:, :head_dim] / total).astype(jnp.bfloat16)
        rest = peak + jnp.log2(total)
        for part in range(PARTS):
            term = rest.astype(jnp.bfloat16).astype(jnp.float32)
            tail = jnp.where(lane == pair * PARTS + part, term, tail)
            rest = rest - term
        for i in range(len(ks)):
            outs[i][pair * row_dev : (pair + 1) * row_dev] = out[i * row_dev : (i + 1) * row_dev]
    for i in range(len(ks)):
        folded = dims.fold(tail[i * row_dev : (i + 1) * row_dev])
        outs[i][dims.pairs * row_dev :] = folded.astype(jnp.bfloat16)


def attend(dims, ks, blocks):
    keys = [key for key in blocks if key[1] != (0,) or key[0] in ks]
    block = jax.ShapeDtypeStruct((dims.back_rows, dims.head_dim), jnp.bfloat16)
    return pl.pallas_call(
        functools.partial(attend_kernel, dims, ks, keys),
        out_shape=[block] * len(ks),
        in_specs=[VMEM] * len(keys),
        out_specs=[VMEM] * len(ks),
        compiler_params=PARAMS,
        cost_estimate=pl.CostEstimate(
            flops=6 * dims.pairs * dims.rows * dims.rows * dims.head_dim,
            transcendentals=dims.pairs * dims.rows * dims.rows,
            bytes_accessed=6 * dims.pairs * dims.rows * dims.head_dim,
        ),
        name="attend",
    )(*[blocks[key] for key in keys])


def collect_kernel(dims, kgs, me_ref, mem_ref, lse_ref, *refs):
    ks = [k for kg in kgs for k in dims.partners(kg)]
    blocks = dict(zip(ks, refs))
    out, wide, done, sems = refs[-4:]
    me, head_dim, row_dev, size = me_ref[0], dims.head_dim, dims.row_dev, dims.tail_rows
    span = head_dim // dims.folds

    def one_hot(shape, match):
        row = lax.broadcasted_iota(jnp.int32, shape, 0) % head_dim
        return match(row, lax.broadcasted_iota(jnp.int32, shape, 1)).astype(jnp.bfloat16)

    tails = jnp.concatenate([blocks[k][dims.pairs * row_dev :] for k in ks], axis=0)
    join = one_hot(
        (head_dim, head_dim),
        lambda row, col: (row // span == col // span) & (row % span // PARTS == col % span),
    )
    col_lse = jnp.dot(tails, join, preferred_element_type=jnp.float32)
    mem_lse = jnp.concatenate([lse_ref[k * size : (k + 1) * size] for k in ks], axis=0)
    share = 1.0 / (1.0 + jnp.exp2(mem_lse - col_lse))
    high = share.astype(jnp.bfloat16)
    low = (share - high.astype(jnp.float32)).astype(jnp.bfloat16)
    terms = jnp.concatenate([high, low], axis=1)
    shares = []
    for fold in range(dims.folds):
        pick = one_hot(
            (2 * head_dim, dims.pairs * head_dim),
            lambda row, col: row - fold * span == col // head_dim,
        )
        shares.append(jnp.dot(terms, pick, preferred_element_type=jnp.float32))

    stores = []
    slot = 0
    for i, kg in enumerate(kgs):
        lane = dims.lane(me, kg)
        for j in range(dims.heads_g):
            for k in dims.partners(kg):
                for c in range(dims.cols_g):
                    pair = j * dims.cols_g + c
                    lanes = slice(pair * head_dim, (pair + 1) * head_dim)
                    rows = slice(ks.index(k) * size, (ks.index(k) + 1) * size)
                    part = jnp.concatenate([fold[rows, lanes] for fold in shares], axis=0)
                    at = dims.at(k, pair)
                    mem = mem_ref[at : at + row_dev]
                    col = blocks[k][pair * row_dev : (pair + 1) * row_dev].astype(jnp.float32)
                    to = pl.ds(
                        dims.column(me, k % dims.col_groups, c), row_dev, stride=dims.col_dev
                    )
                    wide[slot, to, :] = mem + part * (col - mem)
            done[i, j] = (
                wide[slot].astype(jnp.bfloat16).reshape(row_dev, dims.col_dev, head_dim)
            )
            at = pl.ds(pl.multiple_of(lane + j * head_dim, 128), head_dim)
            stores.append(
                pltpu.make_async_copy(done.at[i, j], out.at[:, :, at], sems.at[i, j])
            )
            stores[-1].start()
            slot = (slot + 1) % wide.shape[0]
    for store in stores:
        store.wait()


def collect(dims, kgs, me, mem, lse, blocks, out=None):
    shape = (dims.row_dev, dims.col_dev, dims.heads * dims.head_dim)
    operands = (me, mem, lse, *blocks) + (() if out is None else (out,))
    return pl.pallas_call(
        functools.partial(collect_kernel, dims, kgs),
        out_shape=jax.ShapeDtypeStruct(shape, jnp.bfloat16),
        in_specs=[SMEM] + [VMEM] * (2 + len(blocks)) + [HBM] * (out is not None),
        out_specs=HBM,
        scratch_shapes=[
            pltpu.VMEM((4, dims.patches, dims.head_dim), jnp.float32),
            pltpu.VMEM((len(kgs), dims.heads_g) + shape[:2] + (dims.head_dim,), jnp.bfloat16),
            pltpu.SemaphoreType.DMA((len(kgs), dims.heads_g)),
        ],
        input_output_aliases={} if out is None else {len(operands) - 1: 0},
        compiler_params=PARAMS,
        name="collect",
    )(*operands)


def exchange(dims, ks, blocks):
    return [
        lax.ppermute(block, "row", [(i, i ^ k) for i in range(dims.n_row)]) if k else block
        for k, block in zip(ks, blocks)
    ]


def tied(blocks, *others):
    values, others = lax.optimization_barrier((list(blocks.values()), others))
    return (dict(zip(blocks, values)), *others)


def per_device(queries, keys, values, memory_bias):
    row_dev, col_dev, model_width = queries.shape
    n_row, n_col = lax.axis_size("row"), lax.axis_size("col")
    heads = memory_bias.shape[0]
    dims = Dims(n_row, n_col, heads, model_width // heads, row_dev, col_dev)
    me = lax.axis_index("row").astype(jnp.int32).reshape(1)
    args = (queries, keys, values)
    both, asked, every = (1, 2), (0,), (0, 1, 2)
    last = dims.head_groups - 1
    order = (*range(1, dims.head_groups), 0)

    def split(kg):
        return both if kg == last else every

    early = [kg for kg in order if kg not in (last, 0)]
    waves = [
        [(kg, every) for kg in early],
        [(last, both)] + [(0, every)] * (last > 0),
        [(last, asked)],
    ]
    waves = [parts for parts in waves if parts]
    first = (*early[-1:], *([0] if last else []), *early[:-1])
    got, token = {}, me
    for parts in waves:
        sent = spread(dims, parts, token, args)
        token, _ = lax.optimization_barrier((me, list(sent.values())[0]))
        got.update(zip(sent, exchange(dims, [k for k, _ in sent], sent.values())))

    pooled = pool(dims, keys, values)
    band = lax.all_gather(pooled[None], "col", axis=0, tiled=True)
    mem, lse = recall(dims, me, memory_bias, queries, band[:, 0], band[:, 1])

    held = [(k, split(kg)) for kg in order for k in dims.partners(kg)]
    late = [(k, asked) for k in dims.partners(last)]
    blocks, mem, lse = tied({key: got[key] for key in held}, mem, lse)
    home = {}
    ks = [k for kg in first for k in dims.partners(kg)]
    back = list(attend(dims, ks, blocks))
    tie = back
    home.update(zip(ks, exchange(dims, ks, back)))
    late_blocks, _ = tied({key: got[key] for key in late}, tie)
    ks = [k for kg in order if kg not in first for k in dims.partners(kg)]
    back = list(attend(dims, ks, {**blocks, **late_blocks}))
    home.update(zip(ks, exchange(dims, ks, back)))
    out = None
    for kgs in ((*first,), (last,)):
        ks = [k for kg in kgs for k in dims.partners(kg)]
        out = collect(dims, kgs, me, mem, lse, [home[k] for k in ks], out)
    return out


def solution(mesh):
    return jax.shard_map(
        per_device,
        mesh=mesh,
        in_specs=(P("row", "col", None), P("row", "col", None), P("row", "col", None), P()),
        out_specs=P("row", "col", None),
        check_vma=False,
    )
```

```python
import functools
import math

import jax
import jax.numpy as jnp
from jax import lax
from jax.experimental import pallas as pl
from jax.experimental.pallas import tpu as pltpu
from jax.sharding import PartitionSpec as P


LOG2E = 1.4426950408889634
PARTS = 3
NT = (((1,), (1,)), ((), ()))
PARAMS = pltpu.CompilerParams(vmem_limit_bytes=20 * 1024 * 1024)
SMEM = pl.BlockSpec(memory_space=pltpu.SMEM)
VMEM = pl.BlockSpec(memory_space=pltpu.VMEM)
HBM = pl.BlockSpec(memory_space=pltpu.HBM)


def in_hbm(x):
    return pltpu.with_memory_space_constraint(x, pltpu.HBM)


class Dims:
    def __init__(self, n_row, n_col, heads, head_dim, row_dev, col_dev):
        self.n_row, self.n_col, self.head_dim = n_row, n_col, head_dim
        self.row_dev, self.col_dev, self.heads = row_dev, col_dev, heads
        self.head_groups = math.gcd(heads, n_row)
        self.col_groups = n_row // self.head_groups
        self.heads_g = heads // self.head_groups
        self.cols_g = col_dev // self.col_groups
        self.pairs = self.heads_g * self.cols_g
        self.width = self.heads_g * head_dim
        self.patches = row_dev * col_dev
        self.rows = n_row * row_dev
        self.folds = 2 if 2 * PARTS * self.pairs <= head_dim and row_dev % 32 == 0 else 1
        self.tail_rows = row_dev // self.folds
        self.back_rows = self.pairs * row_dev + self.tail_rows

    def lane(self, me, kg):
        return pl.multiple_of(((me // self.col_groups) ^ kg) * self.width, 128)

    def fold_lanes(self, lane, row_dev):
        row = lax.broadcasted_iota(jnp.int32, lane.shape, 0) % row_dev
        return lane - row // self.tail_rows * (self.head_dim // self.folds)

    def fold(self, tail):
        parts = [
            tail[i * self.tail_rows : (i + 1) * self.tail_rows] for i in range(self.folds)
        ]
        return functools.reduce(lambda a, b: a + b, parts)

    def pieces(self, k):
        return ((1, 2), (0,)) if k >= self.n_row - self.col_groups else ((0, 1, 2),)

    def row(self, kinds, kind, pair):
        return (kinds.index(kind) * self.pairs + pair) * self.row_dev

    def partners(self, kg):
        ks = range(kg * self.col_groups, (kg + 1) * self.col_groups)
        return sorted(ks, reverse=kg == 0)

    def at(self, k, pair):
        return (k * self.pairs + pair) * self.row_dev

    def column(self, me, kl, c):
        return ((me % self.col_groups) ^ kl) * self.cols_g + c


def spread_kernel(dims, parts, me_ref, *refs):
    args, outs, raws, (wide, sems) = (
        refs[:3],
        refs[3 : -2 - len(parts)],
        refs[-2 - len(parts) : -2],
        refs[-2:],
    )
    me, head_dim, row_dev = me_ref[0], dims.head_dim, dims.row_dev
    loads = {}
    for i, (kg, kinds) in enumerate(parts):
        for n, kind in enumerate(kinds):
            loads[i, n] = pltpu.make_async_copy(
                args[kind].at[:, :, pl.ds(dims.lane(me, kg), dims.width)],
                raws[i].at[n],
                sems.at[i, n],
            )
            loads[i, n].start()
    slot = 0
    for i, (kg, kinds) in enumerate(parts):
        ks = dims.partners(kg)
        mine, outs = outs[: len(ks)], outs[len(ks) :]
        for n, kind in enumerate(kinds):
            loads[i, n].wait()
            for j in range(dims.heads_g):
                wide[slot] = (
                    raws[i][n, :, :, j * head_dim : (j + 1) * head_dim]
                    .astype(jnp.float32)
                    .reshape(dims.patches, head_dim)
                )
                for k, out in zip(ks, mine):
                    for c in range(dims.cols_g):
                        patch = pl.ds(
                            dims.column(me, k % dims.col_groups, c), row_dev, stride=dims.col_dev
                        )
                        at = dims.row(kinds, kind, j * dims.cols_g + c)
                        out[at : at + row_dev] = wide[slot, patch, :].astype(jnp.bfloat16)
                slot = (slot + 1) % wide.shape[0]


def spread(dims, parts, me, args):
    keys = [(k, kinds) for kg, kinds in parts for k in dims.partners(kg)]
    rows = dims.pairs * dims.row_dev
    blocks = pl.pallas_call(
        functools.partial(spread_kernel, dims, parts),
        out_shape=[
            jax.ShapeDtypeStruct((len(kinds) * rows, dims.head_dim), jnp.bfloat16)
            for _, kinds in keys
        ],
        in_specs=[SMEM] + [HBM] * 3,
        out_specs=[VMEM] * len(keys),
        scratch_shapes=[
            pltpu.VMEM((len(kinds), dims.row_dev, dims.col_dev, dims.width), jnp.bfloat16)
            for _, kinds in parts
        ]
        + [
            pltpu.VMEM((4, dims.patches, dims.head_dim), jnp.float32),
            pltpu.SemaphoreType.DMA((len(parts), 3)),
        ],
        compiler_params=PARAMS,
        name="spread",
    )(me, *[in_hbm(arg) for arg in args])
    return dict(zip(keys, blocks))


def pool_kernel(dims, k_ref, v_ref, out_ref, raw, sems):
    loads = [
        pltpu.make_async_copy(ref, raw.at[i], sems.at[i]) for i, ref in enumerate((k_ref, v_ref))
    ]
    for load in loads:
        load.start()
    for i, load in enumerate(loads):
        load.wait()
        total = jnp.zeros((dims.col_dev, raw.shape[-1]), jnp.float32)
        for r in range(dims.row_dev):
            total = total + raw[i, r].astype(jnp.float32)
        mean = jnp.sum(total, axis=0, keepdims=True) * (1.0 / dims.patches)
        out_ref[i : i + 1] = mean.astype(jnp.bfloat16).astype(jnp.float32)


def pool(dims, keys, values):
    return pl.pallas_call(
        functools.partial(pool_kernel, dims),
        out_shape=jax.ShapeDtypeStruct((2, keys.shape[-1]), jnp.float32),
        in_specs=[HBM] * 2,
        out_specs=VMEM,
        scratch_shapes=[
            pltpu.VMEM((2,) + keys.shape, jnp.bfloat16),
            pltpu.SemaphoreType.DMA((2,)),
        ],
        compiler_params=PARAMS,
        name="pool",
    )(in_hbm(keys), in_hbm(values)).astype(jnp.bfloat16)


def recall_kernel(
    dims, me_ref, bias_ref, q_ref, key_ref, value_ref, out_ref, lse_ref, raw, wide, wide_lse, sem
):
    load = pltpu.make_async_copy(q_ref, raw, sem)
    load.start()
    load.wait()
    me, head_dim, row_dev = me_ref[0], dims.head_dim, dims.row_dev
    scale = LOG2E / math.sqrt(head_dim)
    ones = jnp.ones((dims.n_col, head_dim), jnp.bfloat16)
    column = dims.fold_lanes(lax.broadcasted_iota(jnp.int32, (row_dev, head_dim), 1), row_dev)
    slot = 0
    for kg in range(dims.head_groups):
        lane = dims.lane(me, kg)
        tails = [jnp.zeros((row_dev, head_dim), jnp.float32)] * dims.col_groups
        for j in range(dims.heads_g):
            at = pl.ds(pl.multiple_of(lane + j * head_dim, 128), head_dim)
            query = raw[:, :, at].reshape(dims.patches, head_dim)
            key, value = key_ref[:, at], jnp.concatenate([value_ref[:, at], ones], axis=1)
            bias = bias_ref[((me // dims.col_groups) ^ kg) * dims.heads_g + j] * LOG2E
            score = lax.dot_general(query, key, NT, preferred_element_type=jnp.float32)
            score = score * scale + bias
            peak = jnp.max(score, axis=1, keepdims=True)
            weight = jnp.exp2(score - peak).astype(jnp.bfloat16)
            mixed = jnp.dot(weight, value, preferred_element_type=jnp.float32)
            total = mixed[:, head_dim:]
            wide[slot] = mixed[:, :head_dim] / total
            wide_lse[slot] = peak + jnp.log2(total)
            for kl in range(dims.col_groups):
                for c in range(dims.cols_g):
                    to = dims.at(kg * dims.col_groups + kl, j * dims.cols_g + c)
                    patch = pl.ds(dims.column(me, kl, c), row_dev, stride=dims.col_dev)
                    out_ref[to : to + row_dev] = wide[slot, patch, :]
                    pair = j * dims.cols_g + c
                    tails[kl] = jnp.where(column == pair, wide_lse[slot, patch, :], tails[kl])
            slot = (slot + 1) % wide.shape[0]
        for kl, tail in enumerate(tails):
            to = (kg * dims.col_groups + kl) * dims.tail_rows
            lse_ref[to : to + dims.tail_rows] = dims.fold(tail)


def recall(dims, me, bias, queries, key, value):
    out = jax.ShapeDtypeStruct((dims.heads * dims.patches, dims.head_dim), jnp.float32)
    tails = jax.ShapeDtypeStruct((dims.n_row * dims.tail_rows, dims.head_dim), jnp.float32)
    wide = pltpu.VMEM((4, dims.patches, dims.head_dim), jnp.float32)
    return pl.pallas_call(
        functools.partial(recall_kernel, dims),
        out_shape=[out, tails],
        in_specs=[SMEM] * 2 + [HBM] + [VMEM] * 2,
        out_specs=[VMEM] * 2,
        scratch_shapes=[
            pltpu.VMEM(queries.shape, jnp.bfloat16),
            wide,
            wide,
            pltpu.SemaphoreType.DMA,
        ],
        compiler_params=PARAMS,
        name="recall",
    )(me, bias, in_hbm(queries), key, value)


def attend_kernel(dims, ks, keys, *refs):
    ins, outs = dict(zip(keys, refs)), refs[len(keys) :]
    row_dev, head_dim, rows = dims.row_dev, dims.head_dim, dims.rows
    count = len(ks) * row_dev
    scale = LOG2E / math.sqrt(head_dim)
    ones = jnp.ones((rows, head_dim), jnp.bfloat16)
    lane = dims.fold_lanes(lax.broadcasted_iota(jnp.int32, (count, head_dim), 1), row_dev)
    tail = jnp.zeros((count, head_dim), jnp.float32)

    def gather(kind, pair, sources):
        parts = []
        for k in sources:
            kinds = [piece for piece in dims.pieces(k) if kind in piece][0]
            at = dims.row(kinds, kind, pair)
            parts.append(ins[k, kinds][at : at + row_dev])
        return jnp.concatenate(parts, axis=0)

    for pair in range(dims.pairs):
        query = gather(0, pair, ks)
        key = gather(1, pair, range(dims.n_row))
        value = jnp.concatenate([gather(2, pair, range(dims.n_row)), ones], axis=1)
        score = lax.dot_general(query, key, NT, preferred_element_type=jnp.float32) * scale
        peak = jnp.max(score, axis=1, keepdims=True)
        weight = jnp.exp2(score - peak).astype(jnp.bfloat16)
        mixed = jnp.dot(weight, value, preferred_element_type=jnp.float32)
        total = mixed[:, head_dim:]
        out = (mixed[:, :head_dim] / total).astype(jnp.bfloat16)
        rest = peak + jnp.log2(total)
        for part in range(PARTS):
            term = rest.astype(jnp.bfloat16).astype(jnp.float32)
            tail = jnp.where(lane == pair * PARTS + part, term, tail)
            rest = rest - term
        for i in range(len(ks)):
            outs[i][pair * row_dev : (pair + 1) * row_dev] = out[i * row_dev : (i + 1) * row_dev]
    for i in range(len(ks)):
        folded = dims.fold(tail[i * row_dev : (i + 1) * row_dev])
        outs[i][dims.pairs * row_dev :] = folded.astype(jnp.bfloat16)


def attend(dims, ks, blocks):
    keys = [key for key in blocks if key[1] != (0,) or key[0] in ks]
    block = jax.ShapeDtypeStruct((dims.back_rows, dims.head_dim), jnp.bfloat16)
    return pl.pallas_call(
        functools.partial(attend_kernel, dims, ks, keys),
        out_shape=[block] * len(ks),
        in_specs=[VMEM] * len(keys),
        out_specs=[VMEM] * len(ks),
        compiler_params=PARAMS,
        cost_estimate=pl.CostEstimate(
            flops=6 * dims.pairs * dims.rows * dims.rows * dims.head_dim,
            transcendentals=dims.pairs * dims.rows * dims.rows,
            bytes_accessed=6 * dims.pairs * dims.rows * dims.head_dim,
        ),
        name="attend",
    )(*[blocks[key] for key in keys])


def collect_kernel(dims, kgs, me_ref, mem_ref, lse_ref, *refs):
    ks = [k for kg in kgs for k in dims.partners(kg)]
    blocks = dict(zip(ks, refs))
    out, wide, done, sems = refs[-4:]
    me, head_dim, row_dev, size = me_ref[0], dims.head_dim, dims.row_dev, dims.tail_rows
    span = head_dim // dims.folds

    def one_hot(shape, match):
        row = lax.broadcasted_iota(jnp.int32, shape, 0) % head_dim
        return match(row, lax.broadcasted_iota(jnp.int32, shape, 1)).astype(jnp.bfloat16)

    tails = jnp.concatenate([blocks[k][dims.pairs * row_dev :] for k in ks], axis=0)
    join = one_hot(
        (head_dim, head_dim),
        lambda row, col: (row // span == col // span) & (row % span // PARTS == col % span),
    )
    col_lse = jnp.dot(tails, join, preferred_element_type=jnp.float32)
    mem_lse = jnp.concatenate([lse_ref[k * size : (k + 1) * size] for k in ks], axis=0)
    share = 1.0 / (1.0 + jnp.exp2(mem_lse - col_lse))
    high = share.astype(jnp.bfloat16)
    low = (share - high.astype(jnp.float32)).astype(jnp.bfloat16)
    terms = jnp.concatenate([high, low], axis=1)
    shares = []
    for fold in range(dims.folds):
        pick = one_hot(
            (2 * head_dim, dims.pairs * head_dim),
            lambda row, col: row - fold * span == col // head_dim,
        )
        shares.append(jnp.dot(terms, pick, preferred_element_type=jnp.float32))

    stores = []
    slot = 0
    for i, kg in enumerate(kgs):
        lane = dims.lane(me, kg)
        for j in range(dims.heads_g):
            for k in dims.partners(kg):
                for c in range(dims.cols_g):
                    pair = j * dims.cols_g + c
                    lanes = slice(pair * head_dim, (pair + 1) * head_dim)
                    rows = slice(ks.index(k) * size, (ks.index(k) + 1) * size)
                    part = jnp.concatenate([fold[rows, lanes] for fold in shares], axis=0)
                    at = dims.at(k, pair)
                    mem = mem_ref[at : at + row_dev]
                    col = blocks[k][pair * row_dev : (pair + 1) * row_dev].astype(jnp.float32)
                    to = pl.ds(
                        dims.column(me, k % dims.col_groups, c), row_dev, stride=dims.col_dev
                    )
                    wide[slot, to, :] = mem + part * (col - mem)
            done[i, j] = (
                wide[slot].astype(jnp.bfloat16).reshape(row_dev, dims.col_dev, head_dim)
            )
            at = pl.ds(pl.multiple_of(lane + j * head_dim, 128), head_dim)
            stores.append(
                pltpu.make_async_copy(done.at[i, j], out.at[:, :, at], sems.at[i, j])
            )
            stores[-1].start()
            slot = (slot + 1) % wide.shape[0]
    for store in stores:
        store.wait()


def collect(dims, kgs, me, mem, lse, blocks, out=None):
    shape = (dims.row_dev, dims.col_dev, dims.heads * dims.head_dim)
    operands = (me, mem, lse, *blocks) + (() if out is None else (out,))
    return pl.pallas_call(
        functools.partial(collect_kernel, dims, kgs),
        out_shape=jax.ShapeDtypeStruct(shape, jnp.bfloat16),
        in_specs=[SMEM] + [VMEM] * (2 + len(blocks)) + [HBM] * (out is not None),
        out_specs=HBM,
        scratch_shapes=[
            pltpu.VMEM((4, dims.patches, dims.head_dim), jnp.float32),
            pltpu.VMEM((len(kgs), dims.heads_g) + shape[:2] + (dims.head_dim,), jnp.bfloat16),
            pltpu.SemaphoreType.DMA((len(kgs), dims.heads_g)),
        ],
        input_output_aliases={} if out is None else {len(operands) - 1: 0},
        compiler_params=PARAMS,
        name="collect",
    )(*operands)


def exchange(dims, ks, blocks):
    return [
        lax.ppermute(block, "row", [(i, i ^ k) for i in range(dims.n_row)]) if k else block
        for k, block in zip(ks, blocks)
    ]


def tied(blocks, *others):
    values, others = lax.optimization_barrier((list(blocks.values()), others))
    return (dict(zip(blocks, values)), *others)


def per_device(queries, keys, values, memory_bias):
    row_dev, col_dev, model_width = queries.shape
    n_row, n_col = lax.axis_size("row"), lax.axis_size("col")
    heads = memory_bias.shape[0]
    dims = Dims(n_row, n_col, heads, model_width // heads, row_dev, col_dev)
    me = lax.axis_index("row").astype(jnp.int32).reshape(1)
    args = (queries, keys, values)
    both, asked, every = (1, 2), (0,), (0, 1, 2)
    last = dims.head_groups - 1
    order = (*range(1, dims.head_groups), 0)

    def split(kg):
        return both if kg == last else every

    early = [kg for kg in order if kg not in (last, 0)]
    waves = [
        [(kg, every) for kg in early],
        [(last, both)] + [(0, every)] * (last > 0),
        [(last, asked)],
    ]
    waves = [parts for parts in waves if parts]
    first = (*early[-1:], *([0] if last else []), *early[:-1])
    got, token = {}, me
    for i, parts in enumerate(waves):
        sent = spread(dims, parts, token, args)
        token, _ = lax.optimization_barrier((me, list(sent.values())[0]))
        got.update(zip(sent, exchange(dims, [k for k, _ in sent], sent.values())))
        if i == 1:
            pooled = pool(dims, keys, values)
            band = lax.all_gather(pooled[None], "col", axis=0, tiled=True)
            mem, lse = recall(dims, me, memory_bias, queries, band[:, 0], band[:, 1])
            token, mem, lse = lax.optimization_barrier((token, mem, lse))

    held = [(k, split(kg)) for kg in order for k in dims.partners(kg)]
    late = [(k, asked) for k in dims.partners(last)]
    blocks, mem, lse = tied({key: got[key] for key in held}, mem, lse)
    home = {}
    ks = [k for kg in first for k in dims.partners(kg)]
    back = list(attend(dims, ks, blocks))
    tie = back
    home.update(zip(ks, exchange(dims, ks, back)))
    late_blocks, _ = tied({key: got[key] for key in late}, tie)
    ks = [k for kg in order if kg not in first for k in dims.partners(kg)]
    back = list(attend(dims, ks, {**blocks, **late_blocks}))
    home.update(zip(ks, exchange(dims, ks, back)))
    out = None
    for kgs in ((*first,), (last,)):
        ks = [k for kg in kgs for k in dims.partners(kg)]
        out = collect(dims, kgs, me, mem, lse, [home[k] for k in ks], out)
    return out


def solution(mesh):
    return jax.shard_map(
        per_device,
        mesh=mesh,
        in_specs=(P("row", "col", None), P("row", "col", None), P("row", "col", None), P()),
        out_specs=P("row", "col", None),
        check_vma=False,
    )
```

```python
import functools
import math

import jax
import jax.numpy as jnp
from jax import lax
from jax.experimental import pallas as pl
from jax.experimental.pallas import tpu as pltpu
from jax.sharding import PartitionSpec as P


LOG2E = 1.4426950408889634
PARTS = 3
NT = (((1,), (1,)), ((), ()))
PARAMS = pltpu.CompilerParams(vmem_limit_bytes=20 * 1024 * 1024)
SMEM = pl.BlockSpec(memory_space=pltpu.SMEM)
VMEM = pl.BlockSpec(memory_space=pltpu.VMEM)
HBM = pl.BlockSpec(memory_space=pltpu.HBM)


def in_hbm(x):
    return pltpu.with_memory_space_constraint(x, pltpu.HBM)


class Dims:
    def __init__(self, n_row, n_col, heads, head_dim, row_dev, col_dev):
        self.n_row, self.n_col, self.head_dim = n_row, n_col, head_dim
        self.row_dev, self.col_dev, self.heads = row_dev, col_dev, heads
        self.head_groups = math.gcd(heads, n_row)
        self.col_groups = n_row // self.head_groups
        self.heads_g = heads // self.head_groups
        self.cols_g = col_dev // self.col_groups
        self.pairs = self.heads_g * self.cols_g
        self.width = self.heads_g * head_dim
        self.patches = row_dev * col_dev
        self.rows = n_row * row_dev
        self.folds = 2 if 2 * PARTS * self.pairs <= head_dim and row_dev % 32 == 0 else 1
        self.tail_rows = row_dev // self.folds
        self.back_rows = self.pairs * row_dev + self.tail_rows

    def lane(self, me, kg):
        return pl.multiple_of(((me // self.col_groups) ^ kg) * self.width, 128)

    def fold_lanes(self, lane, row_dev):
        row = lax.broadcasted_iota(jnp.int32, lane.shape, 0) % row_dev
        return lane - row // self.tail_rows * (self.head_dim // self.folds)

    def fold(self, tail):
        parts = [
            tail[i * self.tail_rows : (i + 1) * self.tail_rows] for i in range(self.folds)
        ]
        return functools.reduce(lambda a, b: a + b, parts)

    def pieces(self, k):
        return ((1, 2), (0,)) if k >= self.n_row - self.col_groups else ((0, 1, 2),)

    def row(self, kinds, kind, pair):
        return (kinds.index(kind) * self.pairs + pair) * self.row_dev

    def partners(self, kg):
        ks = range(kg * self.col_groups, (kg + 1) * self.col_groups)
        return sorted(ks, reverse=kg == 0)

    def at(self, k, pair):
        return (k * self.pairs + pair) * self.row_dev

    def column(self, me, kl, c):
        return ((me % self.col_groups) ^ kl) * self.cols_g + c


def spread_kernel(dims, parts, me_ref, *refs):
    args, outs, raws, (wide, sems) = (
        refs[:3],
        refs[3 : -2 - len(parts)],
        refs[-2 - len(parts) : -2],
        refs[-2:],
    )
    me, head_dim, row_dev = me_ref[0], dims.head_dim, dims.row_dev
    loads = {}
    for i, (kg, kinds) in enumerate(parts):
        for n, kind in enumerate(kinds):
            loads[i, n] = pltpu.make_async_copy(
                args[kind].at[:, :, pl.ds(dims.lane(me, kg), dims.width)],
                raws[i].at[n],
                sems.at[i, n],
            )
            loads[i, n].start()
    slot = 0
    for i, (kg, kinds) in enumerate(parts):
        ks = dims.partners(kg)
        mine, outs = outs[: len(ks)], outs[len(ks) :]
        for n, kind in enumerate(kinds):
            loads[i, n].wait()
            for j in range(dims.heads_g):
                wide[slot] = (
                    raws[i][n, :, :, j * head_dim : (j + 1) * head_dim]
                    .astype(jnp.float32)
                    .reshape(dims.patches, head_dim)
                )
                for k, out in zip(ks, mine):
                    for c in range(dims.cols_g):
                        patch = pl.ds(
                            dims.column(me, k % dims.col_groups, c), row_dev, stride=dims.col_dev
                        )
                        at = dims.row(kinds, kind, j * dims.cols_g + c)
                        out[at : at + row_dev] = wide[slot, patch, :].astype(jnp.bfloat16)
                slot = (slot + 1) % wide.shape[0]


def spread(dims, parts, me, args):
    keys = [(k, kinds) for kg, kinds in parts for k in dims.partners(kg)]
    rows = dims.pairs * dims.row_dev
    blocks = pl.pallas_call(
        functools.partial(spread_kernel, dims, parts),
        out_shape=[
            jax.ShapeDtypeStruct((len(kinds) * rows, dims.head_dim), jnp.bfloat16)
            for _, kinds in keys
        ],
        in_specs=[SMEM] + [HBM] * 3,
        out_specs=[VMEM] * len(keys),
        scratch_shapes=[
            pltpu.VMEM((len(kinds), dims.row_dev, dims.col_dev, dims.width), jnp.bfloat16)
            for _, kinds in parts
        ]
        + [
            pltpu.VMEM((4, dims.patches, dims.head_dim), jnp.float32),
            pltpu.SemaphoreType.DMA((len(parts), 3)),
        ],
        compiler_params=PARAMS,
        name="spread",
    )(me, *[in_hbm(arg) for arg in args])
    return dict(zip(keys, blocks))


def pool_kernel(dims, k_ref, v_ref, out_ref, raw, sems):
    loads = [
        pltpu.make_async_copy(ref, raw.at[i], sems.at[i]) for i, ref in enumerate((k_ref, v_ref))
    ]
    for load in loads:
        load.start()
    for i, load in enumerate(loads):
        load.wait()
        total = jnp.zeros((dims.col_dev, raw.shape[-1]), jnp.float32)
        for r in range(dims.row_dev):
            total = total + raw[i, r].astype(jnp.float32)
        mean = jnp.sum(total, axis=0, keepdims=True) * (1.0 / dims.patches)
        out_ref[i : i + 1] = mean.astype(jnp.bfloat16).astype(jnp.float32)


def pool(dims, keys, values):
    return pl.pallas_call(
        functools.partial(pool_kernel, dims),
        out_shape=jax.ShapeDtypeStruct((2, keys.shape[-1]), jnp.float32),
        in_specs=[HBM] * 2,
        out_specs=VMEM,
        scratch_shapes=[
            pltpu.VMEM((2,) + keys.shape, jnp.bfloat16),
            pltpu.SemaphoreType.DMA((2,)),
        ],
        compiler_params=PARAMS,
        name="pool",
    )(in_hbm(keys), in_hbm(values)).astype(jnp.bfloat16)


def recall_kernel(
    dims, me_ref, bias_ref, q_ref, key_ref, value_ref, out_ref, lse_ref, raw, wide, wide_lse, sem
):
    load = pltpu.make_async_copy(q_ref, raw, sem)
    load.start()
    load.wait()
    me, head_dim, row_dev = me_ref[0], dims.head_dim, dims.row_dev
    scale = LOG2E / math.sqrt(head_dim)
    ones = jnp.ones((dims.n_col, head_dim), jnp.bfloat16)
    column = dims.fold_lanes(lax.broadcasted_iota(jnp.int32, (row_dev, head_dim), 1), row_dev)
    slot = 0
    for kg in range(dims.head_groups):
        lane = dims.lane(me, kg)
        tails = [jnp.zeros((row_dev, head_dim), jnp.float32)] * dims.col_groups
        for j in range(dims.heads_g):
            at = pl.ds(pl.multiple_of(lane + j * head_dim, 128), head_dim)
            query = raw[:, :, at].reshape(dims.patches, head_dim)
            key, value = key_ref[:, at], jnp.concatenate([value_ref[:, at], ones], axis=1)
            bias = bias_ref[((me // dims.col_groups) ^ kg) * dims.heads_g + j] * LOG2E
            score = lax.dot_general(query, key, NT, preferred_element_type=jnp.float32)
            score = score * scale + bias
            peak = jnp.max(score, axis=1, keepdims=True)
            weight = jnp.exp2(score - peak).astype(jnp.bfloat16)
            mixed = jnp.dot(weight, value, preferred_element_type=jnp.float32)
            total = mixed[:, head_dim:]
            wide[slot] = mixed[:, :head_dim] / total
            wide_lse[slot] = peak + jnp.log2(total)
            for kl in range(dims.col_groups):
                for c in range(dims.cols_g):
                    to = dims.at(kg * dims.col_groups + kl, j * dims.cols_g + c)
                    patch = pl.ds(dims.column(me, kl, c), row_dev, stride=dims.col_dev)
                    out_ref[to : to + row_dev] = wide[slot, patch, :]
                    pair = j * dims.cols_g + c
                    tails[kl] = jnp.where(column == pair, wide_lse[slot, patch, :], tails[kl])
            slot = (slot + 1) % wide.shape[0]
        for kl, tail in enumerate(tails):
            to = (kg * dims.col_groups + kl) * dims.tail_rows
            lse_ref[to : to + dims.tail_rows] = dims.fold(tail)


def recall(dims, me, bias, queries, key, value):
    out = jax.ShapeDtypeStruct((dims.heads * dims.patches, dims.head_dim), jnp.float32)
    tails = jax.ShapeDtypeStruct((dims.n_row * dims.tail_rows, dims.head_dim), jnp.float32)
    wide = pltpu.VMEM((4, dims.patches, dims.head_dim), jnp.float32)
    return pl.pallas_call(
        functools.partial(recall_kernel, dims),
        out_shape=[out, tails],
        in_specs=[SMEM] * 2 + [HBM] + [VMEM] * 2,
        out_specs=[VMEM] * 2,
        scratch_shapes=[
            pltpu.VMEM(queries.shape, jnp.bfloat16),
            wide,
            wide,
            pltpu.SemaphoreType.DMA,
        ],
        compiler_params=PARAMS,
        name="recall",
    )(me, bias, in_hbm(queries), key, value)


def attend_kernel(dims, ks, keys, *refs):
    ins, outs = dict(zip(keys, refs)), refs[len(keys) :]
    row_dev, head_dim, rows = dims.row_dev, dims.head_dim, dims.rows
    count = len(ks) * row_dev
    scale = LOG2E / math.sqrt(head_dim)
    ones = jnp.ones((rows, head_dim), jnp.bfloat16)
    lane = dims.fold_lanes(lax.broadcasted_iota(jnp.int32, (count, head_dim), 1), row_dev)
    tail = jnp.zeros((count, head_dim), jnp.float32)

    def gather(kind, pair, sources):
        parts = []
        for k in sources:
            kinds = [piece for piece in dims.pieces(k) if kind in piece][0]
            at = dims.row(kinds, kind, pair)
            parts.append(ins[k, kinds][at : at + row_dev])
        return jnp.concatenate(parts, axis=0)

    for pair in range(dims.pairs):
        query = gather(0, pair, ks)
        key = gather(1, pair, range(dims.n_row))
        value = jnp.concatenate([gather(2, pair, range(dims.n_row)), ones], axis=1)
        score = lax.dot_general(query, key, NT, preferred_element_type=jnp.float32) * scale
        peak = jnp.max(score, axis=1, keepdims=True)
        weight = jnp.exp2(score - peak).astype(jnp.bfloat16)
        mixed = jnp.dot(weight, value, preferred_element_type=jnp.float32)
        total = mixed[:, head_dim:]
        out = (mixed[:, :head_dim] / total).astype(jnp.bfloat16)
        rest = peak + jnp.log2(total)
        for part in range(PARTS):
            term = rest.astype(jnp.bfloat16).astype(jnp.float32)
            tail = jnp.where(lane == pair * PARTS + part, term, tail)
            rest = rest - term
        for i in range(len(ks)):
            outs[i][pair * row_dev : (pair + 1) * row_dev] = out[i * row_dev : (i + 1) * row_dev]
    for i in range(len(ks)):
        folded = dims.fold(tail[i * row_dev : (i + 1) * row_dev])
        outs[i][dims.pairs * row_dev :] = folded.astype(jnp.bfloat16)


def attend(dims, ks, blocks):
    keys = [key for key in blocks if key[1] != (0,) or key[0] in ks]
    block = jax.ShapeDtypeStruct((dims.back_rows, dims.head_dim), jnp.bfloat16)
    return pl.pallas_call(
        functools.partial(attend_kernel, dims, ks, keys),
        out_shape=[block] * len(ks),
        in_specs=[VMEM] * len(keys),
        out_specs=[VMEM] * len(ks),
        compiler_params=PARAMS,
        cost_estimate=pl.CostEstimate(
            flops=6 * dims.pairs * dims.rows * dims.rows * dims.head_dim,
            transcendentals=dims.pairs * dims.rows * dims.rows,
            bytes_accessed=6 * dims.pairs * dims.rows * dims.head_dim,
        ),
        name="attend",
    )(*[blocks[key] for key in keys])


def collect_kernel(dims, kgs, me_ref, mem_ref, lse_ref, *refs):
    ks = [k for kg in kgs for k in dims.partners(kg)]
    blocks = dict(zip(ks, refs))
    out, wide, done, sems = refs[-4:]
    me, head_dim, row_dev, size = me_ref[0], dims.head_dim, dims.row_dev, dims.tail_rows
    span = head_dim // dims.folds

    def one_hot(shape, match):
        row = lax.broadcasted_iota(jnp.int32, shape, 0) % head_dim
        return match(row, lax.broadcasted_iota(jnp.int32, shape, 1)).astype(jnp.bfloat16)

    tails = jnp.concatenate([blocks[k][dims.pairs * row_dev :] for k in ks], axis=0)
    join = one_hot(
        (head_dim, head_dim),
        lambda row, col: (row // span == col // span) & (row % span // PARTS == col % span),
    )
    col_lse = jnp.dot(tails, join, preferred_element_type=jnp.float32)
    mem_lse = jnp.concatenate([lse_ref[k * size : (k + 1) * size] for k in ks], axis=0)
    share = 1.0 / (1.0 + jnp.exp2(mem_lse - col_lse))
    high = share.astype(jnp.bfloat16)
    low = (share - high.astype(jnp.float32)).astype(jnp.bfloat16)
    terms = jnp.concatenate([high, low], axis=1)
    shares = []
    for fold in range(dims.folds):
        pick = one_hot(
            (2 * head_dim, dims.pairs * head_dim),
            lambda row, col: row - fold * span == col // head_dim,
        )
        shares.append(jnp.dot(terms, pick, preferred_element_type=jnp.float32))

    stores = []
    slot = 0
    for i, kg in enumerate(kgs):
        lane = dims.lane(me, kg)
        for j in range(dims.heads_g):
            for k in dims.partners(kg):
                for c in range(dims.cols_g):
                    pair = j * dims.cols_g + c
                    lanes = slice(pair * head_dim, (pair + 1) * head_dim)
                    rows = slice(ks.index(k) * size, (ks.index(k) + 1) * size)
                    part = jnp.concatenate([fold[rows, lanes] for fold in shares], axis=0)
                    at = dims.at(k, pair)
                    mem = mem_ref[at : at + row_dev]
                    col = blocks[k][pair * row_dev : (pair + 1) * row_dev].astype(jnp.float32)
                    to = pl.ds(
                        dims.column(me, k % dims.col_groups, c), row_dev, stride=dims.col_dev
                    )
                    wide[slot, to, :] = mem + part * (col - mem)
            done[i, j] = (
                wide[slot].astype(jnp.bfloat16).reshape(row_dev, dims.col_dev, head_dim)
            )
            at = pl.ds(pl.multiple_of(lane + j * head_dim, 128), head_dim)
            stores.append(
                pltpu.make_async_copy(done.at[i, j], out.at[:, :, at], sems.at[i, j])
            )
            stores[-1].start()
            slot = (slot + 1) % wide.shape[0]
    for store in stores:
        store.wait()


def collect(dims, kgs, me, mem, lse, blocks, out=None):
    shape = (dims.row_dev, dims.col_dev, dims.heads * dims.head_dim)
    operands = (me, mem, lse, *blocks) + (() if out is None else (out,))
    return pl.pallas_call(
        functools.partial(collect_kernel, dims, kgs),
        out_shape=jax.ShapeDtypeStruct(shape, jnp.bfloat16),
        in_specs=[SMEM] + [VMEM] * (2 + len(blocks)) + [HBM] * (out is not None),
        out_specs=HBM,
        scratch_shapes=[
            pltpu.VMEM((4, dims.patches, dims.head_dim), jnp.float32),
            pltpu.VMEM((len(kgs), dims.heads_g) + shape[:2] + (dims.head_dim,), jnp.bfloat16),
            pltpu.SemaphoreType.DMA((len(kgs), dims.heads_g)),
        ],
        input_output_aliases={} if out is None else {len(operands) - 1: 0},
        compiler_params=PARAMS,
        name="collect",
    )(*operands)


def exchange(dims, ks, blocks):
    return [
        lax.ppermute(block, "row", [(i, i ^ k) for i in range(dims.n_row)]) if k else block
        for k, block in zip(ks, blocks)
    ]


def tied(blocks, *others):
    values, others = lax.optimization_barrier((list(blocks.values()), others))
    return (dict(zip(blocks, values)), *others)


def per_device(queries, keys, values, memory_bias):
    row_dev, col_dev, model_width = queries.shape
    n_row, n_col = lax.axis_size("row"), lax.axis_size("col")
    heads = memory_bias.shape[0]
    dims = Dims(n_row, n_col, heads, model_width // heads, row_dev, col_dev)
    me = lax.axis_index("row").astype(jnp.int32).reshape(1)
    args = (queries, keys, values)
    both, asked, every = (1, 2), (0,), (0, 1, 2)
    last = dims.head_groups - 1
    order = (*range(1, dims.head_groups), 0)

    def split(kg):
        return both if kg == last else every

    early = [kg for kg in order if kg not in (last, 0)]
    waves = [
        [(kg, every) for kg in early],
        [(last, both)],
        [(last, asked)] + [(0, every)] * (last > 0),
    ]
    waves = [parts for parts in waves if parts]
    first = (*early[-1:], *([0] if last else []), *early[:-1])
    got, token = {}, me
    for i, parts in enumerate(waves):
        sent = spread(dims, parts, token, args)
        token, _ = lax.optimization_barrier((me, list(sent.values())[0]))
        got.update(zip(sent, exchange(dims, [k for k, _ in sent], sent.values())))
        if i == 1:
            pooled = pool(dims, keys, values)
            band = lax.all_gather(pooled[None], "col", axis=0, tiled=True)
            mem, lse = recall(dims, me, memory_bias, queries, band[:, 0], band[:, 1])
            token, mem, lse = lax.optimization_barrier((token, mem, lse))

    held = [(k, split(kg)) for kg in order for k in dims.partners(kg)]
    late = [(k, asked) for k in dims.partners(last)]
    blocks, mem, lse = tied({key: got[key] for key in held}, mem, lse)
    home = {}
    ks = [k for kg in first for k in dims.partners(kg)]
    back = list(attend(dims, ks, blocks))
    tie = back
    home.update(zip(ks, exchange(dims, ks, back)))
    late_blocks, _ = tied({key: got[key] for key in late}, tie)
    ks = [k for kg in order if kg not in first for k in dims.partners(kg)]
    back = list(attend(dims, ks, {**blocks, **late_blocks}))
    home.update(zip(ks, exchange(dims, ks, back)))
    out = None
    for kgs in ((*first,), (last,)):
        ks = [k for kg in kgs for k in dims.partners(kg)]
        out = collect(dims, kgs, me, mem, lse, [home[k] for k in ks], out)
    return out


def solution(mesh):
    return jax.shard_map(
        per_device,
        mesh=mesh,
        in_specs=(P("row", "col", None), P("row", "col", None), P("row", "col", None), P()),
        out_specs=P("row", "col", None),
        check_vma=False,
    )
```

```python
import functools
import math

import jax
import jax.numpy as jnp
from jax import lax
from jax.experimental import pallas as pl
from jax.experimental.pallas import tpu as pltpu
from jax.sharding import PartitionSpec as P


LOG2E = 1.4426950408889634
PARTS = 3
NT = (((1,), (1,)), ((), ()))
PARAMS = pltpu.CompilerParams(vmem_limit_bytes=20 * 1024 * 1024)
SMEM = pl.BlockSpec(memory_space=pltpu.SMEM)
VMEM = pl.BlockSpec(memory_space=pltpu.VMEM)
HBM = pl.BlockSpec(memory_space=pltpu.HBM)


def in_hbm(x):
    return pltpu.with_memory_space_constraint(x, pltpu.HBM)


class Dims:
    def __init__(self, n_row, n_col, heads, head_dim, row_dev, col_dev):
        self.n_row, self.n_col, self.head_dim = n_row, n_col, head_dim
        self.row_dev, self.col_dev, self.heads = row_dev, col_dev, heads
        self.head_groups = math.gcd(heads, n_row)
        self.col_groups = n_row // self.head_groups
        self.heads_g = heads // self.head_groups
        self.cols_g = col_dev // self.col_groups
        self.pairs = self.heads_g * self.cols_g
        self.width = self.heads_g * head_dim
        self.patches = row_dev * col_dev
        self.rows = n_row * row_dev
        self.folds = 2 if 2 * PARTS * self.pairs <= head_dim and row_dev % 32 == 0 else 1
        self.tail_rows = row_dev // self.folds
        self.back_rows = self.pairs * row_dev + self.tail_rows

    def lane(self, me, kg):
        return pl.multiple_of(((me // self.col_groups) ^ kg) * self.width, 128)

    def fold_lanes(self, lane, row_dev):
        row = lax.broadcasted_iota(jnp.int32, lane.shape, 0) % row_dev
        return lane - row // self.tail_rows * (self.head_dim // self.folds)

    def fold(self, tail):
        parts = [
            tail[i * self.tail_rows : (i + 1) * self.tail_rows] for i in range(self.folds)
        ]
        return functools.reduce(lambda a, b: a + b, parts)

    def pieces(self, k):
        return ((1, 2), (0,)) if k >= self.n_row - self.col_groups else ((0, 1, 2),)

    def row(self, kinds, kind, pair):
        return (kinds.index(kind) * self.pairs + pair) * self.row_dev

    def partners(self, kg):
        ks = range(kg * self.col_groups, (kg + 1) * self.col_groups)
        return sorted(ks, reverse=kg == 0)

    def at(self, k, pair):
        return (k * self.pairs + pair) * self.row_dev

    def column(self, me, kl, c):
        return ((me % self.col_groups) ^ kl) * self.cols_g + c


def spread_kernel(dims, parts, me_ref, *refs):
    args, outs, raws, (wide, sems) = (
        refs[:3],
        refs[3 : -2 - len(parts)],
        refs[-2 - len(parts) : -2],
        refs[-2:],
    )
    me, head_dim, row_dev = me_ref[0], dims.head_dim, dims.row_dev
    loads = {}
    for i, (kg, kinds) in enumerate(parts):
        for n, kind in enumerate(kinds):
            for j in range(dims.heads_g):
                lane = pl.multiple_of(dims.lane(me, kg) + j * head_dim, 128)
                loads[i, n, j] = pltpu.make_async_copy(
                    args[kind].at[:, :, pl.ds(lane, head_dim)],
                    raws[i].at[n, :, :, pl.ds(j * head_dim, head_dim)],
                    sems.at[i, n, j],
                )
                loads[i, n, j].start()
    slot = 0
    for i, (kg, kinds) in enumerate(parts):
        ks = dims.partners(kg)
        mine, outs = outs[: len(ks)], outs[len(ks) :]
        for n, kind in enumerate(kinds):
            for j in range(dims.heads_g):
                loads[i, n, j].wait()
                wide[slot] = (
                    raws[i][n, :, :, j * head_dim : (j + 1) * head_dim]
                    .astype(jnp.float32)
                    .reshape(dims.patches, head_dim)
                )
                for k, out in zip(ks, mine):
                    for c in range(dims.cols_g):
                        patch = pl.ds(
                            dims.column(me, k % dims.col_groups, c), row_dev, stride=dims.col_dev
                        )
                        at = dims.row(kinds, kind, j * dims.cols_g + c)
                        out[at : at + row_dev] = wide[slot, patch, :].astype(jnp.bfloat16)
                slot = (slot + 1) % wide.shape[0]


def spread(dims, parts, me, args):
    keys = [(k, kinds) for kg, kinds in parts for k in dims.partners(kg)]
    rows = dims.pairs * dims.row_dev
    blocks = pl.pallas_call(
        functools.partial(spread_kernel, dims, parts),
        out_shape=[
            jax.ShapeDtypeStruct((len(kinds) * rows, dims.head_dim), jnp.bfloat16)
            for _, kinds in keys
        ],
        in_specs=[SMEM] + [HBM] * 3,
        out_specs=[VMEM] * len(keys),
        scratch_shapes=[
            pltpu.VMEM((len(kinds), dims.row_dev, dims.col_dev, dims.width), jnp.bfloat16)
            for _, kinds in parts
        ]
        + [
            pltpu.VMEM((4, dims.patches, dims.head_dim), jnp.float32),
            pltpu.SemaphoreType.DMA((len(parts), 3, dims.heads_g)),
        ],
        compiler_params=PARAMS,
        name="spread",
    )(me, *[in_hbm(arg) for arg in args])
    return dict(zip(keys, blocks))


def pool_kernel(dims, k_ref, v_ref, out_ref, raw, sems):
    loads = [
        pltpu.make_async_copy(ref, raw.at[i], sems.at[i]) for i, ref in enumerate((k_ref, v_ref))
    ]
    for load in loads:
        load.start()
    for i, load in enumerate(loads):
        load.wait()
        total = jnp.zeros((dims.col_dev, raw.shape[-1]), jnp.float32)
        for r in range(dims.row_dev):
            total = total + raw[i, r].astype(jnp.float32)
        mean = jnp.sum(total, axis=0, keepdims=True) * (1.0 / dims.patches)
        out_ref[i : i + 1] = mean.astype(jnp.bfloat16).astype(jnp.float32)


def pool(dims, keys, values):
    return pl.pallas_call(
        functools.partial(pool_kernel, dims),
        out_shape=jax.ShapeDtypeStruct((2, keys.shape[-1]), jnp.float32),
        in_specs=[HBM] * 2,
        out_specs=VMEM,
        scratch_shapes=[
            pltpu.VMEM((2,) + keys.shape, jnp.bfloat16),
            pltpu.SemaphoreType.DMA((2,)),
        ],
        compiler_params=PARAMS,
        name="pool",
    )(in_hbm(keys), in_hbm(values)).astype(jnp.bfloat16)


def recall_kernel(
    dims, me_ref, bias_ref, q_ref, key_ref, value_ref, out_ref, lse_ref, raw, wide, wide_lse, sem
):
    load = pltpu.make_async_copy(q_ref, raw, sem)
    load.start()
    load.wait()
    me, head_dim, row_dev = me_ref[0], dims.head_dim, dims.row_dev
    scale = LOG2E / math.sqrt(head_dim)
    ones = jnp.ones((dims.n_col, head_dim), jnp.bfloat16)
    column = dims.fold_lanes(lax.broadcasted_iota(jnp.int32, (row_dev, head_dim), 1), row_dev)
    slot = 0
    for kg in range(dims.head_groups):
        lane = dims.lane(me, kg)
        tails = [jnp.zeros((row_dev, head_dim), jnp.float32)] * dims.col_groups
        for j in range(dims.heads_g):
            at = pl.ds(pl.multiple_of(lane + j * head_dim, 128), head_dim)
            query = raw[:, :, at].reshape(dims.patches, head_dim)
            key, value = key_ref[:, at], jnp.concatenate([value_ref[:, at], ones], axis=1)
            bias = bias_ref[((me // dims.col_groups) ^ kg) * dims.heads_g + j] * LOG2E
            score = lax.dot_general(query, key, NT, preferred_element_type=jnp.float32)
            score = score * scale + bias
            peak = jnp.max(score, axis=1, keepdims=True)
            weight = jnp.exp2(score - peak).astype(jnp.bfloat16)
            mixed = jnp.dot(weight, value, preferred_element_type=jnp.float32)
            total = mixed[:, head_dim:]
            wide[slot] = mixed[:, :head_dim] / total
            wide_lse[slot] = peak + jnp.log2(total)
            for kl in range(dims.col_groups):
                for c in range(dims.cols_g):
                    to = dims.at(kg * dims.col_groups + kl, j * dims.cols_g + c)
                    patch = pl.ds(dims.column(me, kl, c), row_dev, stride=dims.col_dev)
                    out_ref[to : to + row_dev] = wide[slot, patch, :]
                    pair = j * dims.cols_g + c
                    tails[kl] = jnp.where(column == pair, wide_lse[slot, patch, :], tails[kl])
            slot = (slot + 1) % wide.shape[0]
        for kl, tail in enumerate(tails):
            to = (kg * dims.col_groups + kl) * dims.tail_rows
            lse_ref[to : to + dims.tail_rows] = dims.fold(tail)


def recall(dims, me, bias, queries, key, value):
    out = jax.ShapeDtypeStruct((dims.heads * dims.patches, dims.head_dim), jnp.float32)
    tails = jax.ShapeDtypeStruct((dims.n_row * dims.tail_rows, dims.head_dim), jnp.float32)
    wide = pltpu.VMEM((4, dims.patches, dims.head_dim), jnp.float32)
    return pl.pallas_call(
        functools.partial(recall_kernel, dims),
        out_shape=[out, tails],
        in_specs=[SMEM] * 2 + [HBM] + [VMEM] * 2,
        out_specs=[VMEM] * 2,
        scratch_shapes=[
            pltpu.VMEM(queries.shape, jnp.bfloat16),
            wide,
            wide,
            pltpu.SemaphoreType.DMA,
        ],
        compiler_params=PARAMS,
        name="recall",
    )(me, bias, in_hbm(queries), key, value)


def attend_kernel(dims, ks, keys, *refs):
    ins, outs = dict(zip(keys, refs)), refs[len(keys) :]
    row_dev, head_dim, rows = dims.row_dev, dims.head_dim, dims.rows
    count = len(ks) * row_dev
    scale = LOG2E / math.sqrt(head_dim)
    ones = jnp.ones((rows, head_dim), jnp.bfloat16)
    lane = dims.fold_lanes(lax.broadcasted_iota(jnp.int32, (count, head_dim), 1), row_dev)
    tail = jnp.zeros((count, head_dim), jnp.float32)

    def gather(kind, pair, sources):
        parts = []
        for k in sources:
            kinds = [piece for piece in dims.pieces(k) if kind in piece][0]
            at = dims.row(kinds, kind, pair)
            parts.append(ins[k, kinds][at : at + row_dev])
        return jnp.concatenate(parts, axis=0)

    for pair in range(dims.pairs):
        query = gather(0, pair, ks)
        key = gather(1, pair, range(dims.n_row))
        value = jnp.concatenate([gather(2, pair, range(dims.n_row)), ones], axis=1)
        score = lax.dot_general(query, key, NT, preferred_element_type=jnp.float32) * scale
        peak = jnp.max(score, axis=1, keepdims=True)
        weight = jnp.exp2(score - peak).astype(jnp.bfloat16)
        mixed = jnp.dot(weight, value, preferred_element_type=jnp.float32)
        total = mixed[:, head_dim:]
        out = (mixed[:, :head_dim] / total).astype(jnp.bfloat16)
        rest = peak + jnp.log2(total)
        for part in range(PARTS):
            term = rest.astype(jnp.bfloat16).astype(jnp.float32)
            tail = jnp.where(lane == pair * PARTS + part, term, tail)
            rest = rest - term
        for i in range(len(ks)):
            outs[i][pair * row_dev : (pair + 1) * row_dev] = out[i * row_dev : (i + 1) * row_dev]
    for i in range(len(ks)):
        folded = dims.fold(tail[i * row_dev : (i + 1) * row_dev])
        outs[i][dims.pairs * row_dev :] = folded.astype(jnp.bfloat16)


def attend(dims, ks, blocks):
    keys = [key for key in blocks if key[1] != (0,) or key[0] in ks]
    block = jax.ShapeDtypeStruct((dims.back_rows, dims.head_dim), jnp.bfloat16)
    return pl.pallas_call(
        functools.partial(attend_kernel, dims, ks, keys),
        out_shape=[block] * len(ks),
        in_specs=[VMEM] * len(keys),
        out_specs=[VMEM] * len(ks),
        compiler_params=PARAMS,
        cost_estimate=pl.CostEstimate(
            flops=6 * dims.pairs * dims.rows * dims.rows * dims.head_dim,
            transcendentals=dims.pairs * dims.rows * dims.rows,
            bytes_accessed=6 * dims.pairs * dims.rows * dims.head_dim,
        ),
        name="attend",
    )(*[blocks[key] for key in keys])


def collect_kernel(dims, kgs, me_ref, mem_ref, lse_ref, *refs):
    ks = [k for kg in kgs for k in dims.partners(kg)]
    blocks = dict(zip(ks, refs))
    out, wide, done, sems = refs[-4:]
    me, head_dim, row_dev, size = me_ref[0], dims.head_dim, dims.row_dev, dims.tail_rows
    span = head_dim // dims.folds

    def one_hot(shape, match):
        row = lax.broadcasted_iota(jnp.int32, shape, 0) % head_dim
        return match(row, lax.broadcasted_iota(jnp.int32, shape, 1)).astype(jnp.bfloat16)

    tails = jnp.concatenate([blocks[k][dims.pairs * row_dev :] for k in ks], axis=0)
    join = one_hot(
        (head_dim, head_dim),
        lambda row, col: (row // span == col // span) & (row % span // PARTS == col % span),
    )
    col_lse = jnp.dot(tails, join, preferred_element_type=jnp.float32)
    mem_lse = jnp.concatenate([lse_ref[k * size : (k + 1) * size] for k in ks], axis=0)
    share = 1.0 / (1.0 + jnp.exp2(mem_lse - col_lse))
    high = share.astype(jnp.bfloat16)
    low = (share - high.astype(jnp.float32)).astype(jnp.bfloat16)
    terms = jnp.concatenate([high, low], axis=1)
    shares = []
    for fold in range(dims.folds):
        pick = one_hot(
            (2 * head_dim, dims.pairs * head_dim),
            lambda row, col: row - fold * span == col // head_dim,
        )
        shares.append(jnp.dot(terms, pick, preferred_element_type=jnp.float32))

    stores = []
    slot = 0
    for i, kg in enumerate(kgs):
        lane = dims.lane(me, kg)
        for j in range(dims.heads_g):
            for k in dims.partners(kg):
                for c in range(dims.cols_g):
                    pair = j * dims.cols_g + c
                    lanes = slice(pair * head_dim, (pair + 1) * head_dim)
                    rows = slice(ks.index(k) * size, (ks.index(k) + 1) * size)
                    part = jnp.concatenate([fold[rows, lanes] for fold in shares], axis=0)
                    at = dims.at(k, pair)
                    mem = mem_ref[at : at + row_dev]
                    col = blocks[k][pair * row_dev : (pair + 1) * row_dev].astype(jnp.float32)
                    to = pl.ds(
                        dims.column(me, k % dims.col_groups, c), row_dev, stride=dims.col_dev
                    )
                    wide[slot, to, :] = mem + part * (col - mem)
            done[i, j] = (
                wide[slot].astype(jnp.bfloat16).reshape(row_dev, dims.col_dev, head_dim)
            )
            at = pl.ds(pl.multiple_of(lane + j * head_dim, 128), head_dim)
            stores.append(
                pltpu.make_async_copy(done.at[i, j], out.at[:, :, at], sems.at[i, j])
            )
            stores[-1].start()
            slot = (slot + 1) % wide.shape[0]
    for store in stores:
        store.wait()


def collect(dims, kgs, me, mem, lse, blocks, out=None):
    shape = (dims.row_dev, dims.col_dev, dims.heads * dims.head_dim)
    operands = (me, mem, lse, *blocks) + (() if out is None else (out,))
    return pl.pallas_call(
        functools.partial(collect_kernel, dims, kgs),
        out_shape=jax.ShapeDtypeStruct(shape, jnp.bfloat16),
        in_specs=[SMEM] + [VMEM] * (2 + len(blocks)) + [HBM] * (out is not None),
        out_specs=HBM,
        scratch_shapes=[
            pltpu.VMEM((4, dims.patches, dims.head_dim), jnp.float32),
            pltpu.VMEM((len(kgs), dims.heads_g) + shape[:2] + (dims.head_dim,), jnp.bfloat16),
            pltpu.SemaphoreType.DMA((len(kgs), dims.heads_g)),
        ],
        input_output_aliases={} if out is None else {len(operands) - 1: 0},
        compiler_params=PARAMS,
        name="collect",
    )(*operands)


def exchange(dims, ks, blocks):
    return [
        lax.ppermute(block, "row", [(i, i ^ k) for i in range(dims.n_row)]) if k else block
        for k, block in zip(ks, blocks)
    ]


def tied(blocks, *others):
    values, others = lax.optimization_barrier((list(blocks.values()), others))
    return (dict(zip(blocks, values)), *others)


def per_device(queries, keys, values, memory_bias):
    row_dev, col_dev, model_width = queries.shape
    n_row, n_col = lax.axis_size("row"), lax.axis_size("col")
    heads = memory_bias.shape[0]
    dims = Dims(n_row, n_col, heads, model_width // heads, row_dev, col_dev)
    me = lax.axis_index("row").astype(jnp.int32).reshape(1)
    args = (queries, keys, values)
    both, asked, every = (1, 2), (0,), (0, 1, 2)
    last = dims.head_groups - 1
    order = (*range(1, dims.head_groups), 0)

    def split(kg):
        return both if kg == last else every

    early = [kg for kg in order if kg not in (last, 0)]
    waves = [
        [(kg, every) for kg in early],
        [(last, both)] + [(0, every)] * (last > 0),
        [(last, asked)],
    ]
    waves = [parts for parts in waves if parts]
    first = (*early[-1:], *([0] if last else []), *early[:-1])
    got, token = {}, me
    for i, parts in enumerate(waves):
        sent = spread(dims, parts, token, args)
        token, _ = lax.optimization_barrier((me, list(sent.values())[0]))
        got.update(zip(sent, exchange(dims, [k for k, _ in sent], sent.values())))
        if i == 1:
            pooled = pool(dims, keys, values)
            band = lax.all_gather(pooled[None], "col", axis=0, tiled=True)
            mem, lse = recall(dims, me, memory_bias, queries, band[:, 0], band[:, 1])
            token, mem, lse = lax.optimization_barrier((token, mem, lse))

    held = [(k, split(kg)) for kg in order for k in dims.partners(kg)]
    late = [(k, asked) for k in dims.partners(last)]
    blocks, mem, lse = tied({key: got[key] for key in held}, mem, lse)
    home = {}
    ks = [k for kg in first for k in dims.partners(kg)]
    back = list(attend(dims, ks, blocks))
    tie = back
    home.update(zip(ks, exchange(dims, ks, back)))
    late_blocks, _ = tied({key: got[key] for key in late}, tie)
    ks = [k for kg in order if kg not in first for k in dims.partners(kg)]
    back = list(attend(dims, ks, {**blocks, **late_blocks}))
    home.update(zip(ks, exchange(dims, ks, back)))
    out = None
    for kgs in ((*first,), (last,)):
        ks = [k for kg in kgs for k in dims.partners(kg)]
        out = collect(dims, kgs, me, mem, lse, [home[k] for k in ks], out)
    return out


def solution(mesh):
    return jax.shard_map(
        per_device,
        mesh=mesh,
        in_specs=(P("row", "col", None), P("row", "col", None), P("row", "col", None), P()),
        out_specs=P("row", "col", None),
        check_vma=False,
    )
```
